128 devices in a mesh: ctx: 32 (over z, x, core), exp: 4 (over y).
Axes of the slice: x: 4, y: 4, z: 4, core: 2. Of those that a mesh axis runs over, the one named last changes fastest.
Arguments:
- queries: bfloat16 [4096, 6144], P('ctx', 'exp'), may hold values from -6 to 6
- keys: bfloat16 [4096, 6144], P('ctx', 'exp'), may hold values from -6 to 6
- values: bfloat16 [4096, 6144], P('ctx', 'exp'), may hold values from -6 to 6
- out_grad: bfloat16 [4096, 6144], P('ctx', 'exp'), may hold values from -6 to 6
- up_weight: bfloat16 [32, 6144, 2304], P('ctx', 'exp'), may hold values from -0.078125 to 0.078125
- down_weight: bfloat16 [32, 2304, 6144], P('ctx', None, 'exp'), may hold values from -0.09375 to 0.09375
- decay_rates: float32 [48], P('exp'), may hold values from 2.4414063e-05 to 0.0333333333
- routes: int32 [4096, 2], P('ctx'), may hold values from 0 to 15, all different within a row; in each aligned block of 128 rows (0 to 127, 128 to 255, ...) at most 18 rows name the same one
- gate_weights: float32 [4096, 2], P('ctx'), may hold values from 0.1 to 1
Outputs:
- query_grad: bfloat16 [4096, 6144], P('ctx', 'exp')
- key_grad: bfloat16 [4096, 6144], P('ctx', 'exp')
- value_grad: bfloat16 [4096, 6144], P('ctx', 'exp')
The draws below stay inside these ranges and needn't reach their ends.
Inputs may be any that keep to these rules, and one draw needn't show every extreme that they name: `routes`: in each aligned block of 128 tokens a token's two experts differ and no expert is named by more than 18 tokens; in every draw some expert is named by exactly 18 tokens of some block.
All inputs are finite; a program needn't handle non-finite values.
Results may differ from the reference program's by a relative error of at most 0.0117.
Values may be sent and summed in bfloat16 or wider, within the bound.
A program may use at most 128 MiB of HBM per device.

```python
import math
import jax
import jax.numpy as jnp
import numpy as np
from jax import lax

H = 48
DH = 128
D = 6144
FF = 4608
TOK_CTX = 128
TOKENS = 4096
EXPERTS = 16
CAP = 18
N_CTX = 32
N_EXP = 4


def draw_decay_rates(key, part):
    pick_key = jax.random.fold_in(key, 11)
    slow_key = jax.random.fold_in(key, 12)
    fast_key = jax.random.fold_in(key, 13)
    fast_share = 0.5
    slow_low = 0.2 / TOKENS
    slow_high = 2.0 / TOKENS
    slow_rates = jnp.exp(jax.random.uniform(slow_key, (H,), jnp.float32, minval=math.log(slow_low), maxval=math.log(slow_high)))
    fast_rates = jnp.exp(jax.random.uniform(fast_key, (H,), jnp.float32, minval=math.log(1.0 / 50.0), maxval=math.log(1.0 / 30.0)))
    chosen = jax.random.uniform(pick_key, (H,), jnp.float32) < fast_share
    return jnp.where(chosen, fast_rates, slow_rates).astype(jnp.float32)


def level_of(key, dims, split, smallest, largest):
    gain, own = 1.0, jax.random.fold_in(key, 6)
    for dim, parts in split:
        heights = jnp.exp(jax.random.uniform(jax.random.fold_in(own, dim), (parts,), jnp.float32, smallest / len(split), largest / len(split)))
        gain = gain * jnp.repeat(heights, dims[dim] // parts).reshape([-1 if axis == dim else 1 for axis in range(len(dims))])
    return gain


def routed_block(stream_key, own, number, rows, amount, top, limit, lean):
    sequence = jax.random.permutation(stream_key, amount)
    packed, ordinary = portions_of(amount, rows * top, limit, lean, True), portions_of(amount, rows * top, limit, lean, False)
    places = jnp.arange(amount)

    def named(lengths, offset_by):
        used = int((lengths > 0).sum())
        fixed = max(1, used // 4)
        shifted = fixed + (places - fixed + offset_by * (used - fixed)) % max(1, amount - fixed)
        return jnp.zeros((amount,), jnp.int32).at[sequence[jnp.where(places < fixed, places, shifted)]].set(jnp.asarray(lengths, jnp.int32))

    lengths = jnp.where(number % 4 == 0, named(packed, number // 4), named(ordinary, number - number // 4 - 1))
    mixed = jax.random.permutation(jax.random.fold_in(own, 3), amount)
    donor, taker = mixed[0:amount // 2 * 2:2], mixed[1:amount // 2 * 2:2]
    slack = jnp.minimum(lengths[donor] - 1, limit - lengths[taker]) // 2
    slack = jnp.where((donor == sequence[0]) | (taker == sequence[0]) | (lengths[taker] == 0), 0, jnp.maximum(slack, 0))
    shifted = jax.random.randint(jax.random.fold_in(own, 4), (amount // 2,), 0, 1 << 20) % (slack + 1)
    lengths = lengths.at[donor].add(-shifted).at[taker].add(shifted)
    labels = jnp.searchsorted(jnp.cumsum(lengths), jnp.arange(rows * top), side="right").astype(jnp.int32)
    listing = labels.reshape(top, rows).T
    listing = listing[jax.random.permutation(jax.random.fold_in(own, 1), rows)]
    offset_by = jax.random.randint(jax.random.fold_in(own, 2), (rows, 1), 0, top)
    return jnp.take_along_axis(listing, (jnp.arange(top)[None, :] + offset_by) % top, axis=1)


def portions_of(amount, total, limit, skew, full):
    loads = [(1 << 20) // math.isqrt(grade ** skew) + 1 for grade in range(1, amount + 1)]
    largest = limit if full else min(limit, max(-(-total // amount), total * loads[0] // sum(loads)))
    least = 1 if total - largest >= amount - 1 else 0
    given, rest = [largest] + [least] * (amount - 1), total - largest - least * (amount - 1)
    while rest > 0:
        candidates = [i for i in range(1, amount) if given[i] < largest] or [i for i in range(1, amount) if given[i] < limit]
        whole, budget = sum([loads[i] for i in candidates]), rest
        for i in candidates:
            addition = min(limit - given[i], max(1, budget * loads[i] // whole), rest)
            given[i] = given[i] + addition
            rest = rest - addition
    return np.array(given)


def scatter_about(stream_key, shape, spread, limit, split=(), kind=jnp.bfloat16):
    entries = spread * jax.random.normal(stream_key, shape, jnp.float32)
    if split:
        entries = entries * level_of(stream_key, shape, split, -0.22, 0.18)
    return jnp.clip(entries, -limit, limit).astype(kind)


def setup_inputs(seed: int = 0) -> dict:
    streams_of = jax.random.split(jax.random.key(seed), 10)
    queries = scatter_about(streams_of[0], (TOKENS, D), 1.0, 6.0, ((0, 32), (1, 4)))
    keys = scatter_about(streams_of[1], (TOKENS, D), 1.0, 6.0, ((0, 32), (1, 4)))
    values = scatter_about(streams_of[2], (TOKENS, D), 1.0, 6.0, ((0, 32), (1, 4)))
    out_grad = scatter_about(streams_of[3], (TOKENS, D), 1.0, 6.0, ((0, 32), (1, 4)))
    up_weight = scatter_about(streams_of[4], (2 * EXPERTS, D, FF // 2), D ** -0.5, 0.078125, ((0, 32), (1, 4)))
    down_weight = scatter_about(streams_of[5], (2 * EXPERTS, FF // 2, D), FF ** -0.5, 0.09375, ((0, 32), (2, 4)))
    decay_rates = draw_decay_rates(jax.random.fold_in(streams_of[9], 71), 0)
    routes_keys = jax.random.split(jax.random.fold_in(streams_of[7], 1), TOKENS // TOK_CTX)
    routes_turns = jax.random.permutation(jax.random.fold_in(streams_of[7], 3), TOKENS // TOK_CTX)
    routes = jax.vmap(lambda own, number: routed_block(jax.random.fold_in(streams_of[7], 2), own, number, TOK_CTX, EXPERTS, 2, CAP, 2))(routes_keys, routes_turns).reshape((TOKENS, 2))
    gate_weights = jnp.clip(0.1 + 0.9 * jax.random.uniform(streams_of[8], (TOKENS, 2), jnp.float32) ** level_of(streams_of[8], (TOKENS, 2), ((0, 32),), -0.2, 0.2), 0.1, 1.0)
    return dict(queries=queries, keys=keys, values=values, out_grad=out_grad, up_weight=up_weight, down_weight=down_weight, decay_rates=decay_rates, routes=routes, gate_weights=gate_weights)


HIGHEST = lax.Precision.HIGHEST

def silu_slope(value):
    sigma = jax.nn.sigmoid(value)
    return sigma * (1.0 + value * (1.0 - sigma))

def decay_tables(rates, block_len):
    offsets = jnp.arange(block_len).astype(jnp.float32)
    distance = offsets[:, None] - offsets[None, :]
    within = jnp.where(distance[None] >= 0.0, jnp.exp(-rates[:, None, None] * jnp.maximum(distance, 0.0)[None]), 0.0)
    start_pow = jnp.exp(-rates[None, :] * offsets[:, None])
    end_pow = jnp.exp(-rates[None, :] * (block_len - offsets)[:, None])
    last_pow = jnp.exp(-rates[None, :] * (block_len - 1.0 - offsets)[:, None])
    next_pow = jnp.exp(-rates[None, :] * (offsets + 1.0)[:, None])
    whole_pow = jnp.exp(-rates * block_len)
    return (within, start_pow, end_pow, last_pow, next_pow, whole_pow)

def slot_tables(route_block, gate_block, experts, capacity):
    flat = route_block.reshape(-1).astype(jnp.int32)
    hits = (flat[:, None] == jnp.arange(experts, dtype=jnp.int32)[None, :]).astype(jnp.int32)
    before = jnp.cumsum(hits, axis=0) - hits
    placed = lax.optimization_barrier(jnp.sum(before * hits, axis=1))
    target = flat * capacity + placed
    match = (target[None, :] == jnp.arange(experts * capacity, dtype=jnp.int32)[:, None]).astype(jnp.float32)
    match = match.reshape(experts * capacity, route_block.shape[0], route_block.shape[1])
    return (lax.optimization_barrier(jnp.sum(match, axis=2)), lax.optimization_barrier(jnp.sum(match * gate_block[None].astype(jnp.float32), axis=2)))

def reference(queries, keys, values, out_grad, up_weight, down_weight, decay_rates, routes, gate_weights):
    scale = 1.0 / DH
    blocks = N_CTX
    block_len = TOK_CTX
    group = D // N_EXP
    half_ff = FF // 2
    within, start_pow, end_pow, last_pow, next_pow, whole_pow = decay_tables(decay_rates, block_len)

    def blocked(array):
        return array.reshape(blocks, block_len, H, DH)

    def forward_step(state, items):
        query_blk, key_blk, value_blk = items
        query_wide = query_blk.astype(jnp.float32)
        key_wide = key_blk.astype(jnp.float32)
        value_wide = value_blk.astype(jnp.float32)
        scores = jnp.einsum('ihd,jhd->hij', query_wide, key_wide)
        weights = (scale * scores * within).astype(jnp.bfloat16)
        intra = jnp.einsum('hij,jhd->ihd', weights.astype(jnp.float32), value_wide)
        inter = scale * start_pow[:, :, None] * jnp.einsum('ihd,hde->ihe', query_wide, state, precision=HIGHEST)
        local = jnp.einsum('ihd,ihe->hde', key_wide * end_pow[:, :, None], value_wide, precision=HIGHEST)
        return (whole_pow[:, None, None] * state + local, ((intra + inter).astype(jnp.bfloat16), state))
    zero_state = jnp.zeros((H, DH, DH), jnp.float32)
    unused, (attn_out, entering) = lax.scan(forward_step, zero_state, (blocked(queries), blocked(keys), blocked(values)))
    choose, weigh = jax.vmap(lambda route_block, gate_block: slot_tables(route_block, gate_block, EXPERTS, CAP))(routes.reshape(blocks, block_len, 2), gate_weights.reshape(blocks, block_len, 2))

    def gather_rows(rows):
        buffer = jnp.einsum('bsl,bld->bsd', choose, rows.reshape(blocks, block_len, D).astype(jnp.float32))
        buffer = buffer.astype(jnp.bfloat16).reshape(blocks, EXPERTS, CAP, D)
        return buffer.transpose(1, 0, 2, 3).reshape(EXPERTS, blocks * CAP, D)

    def expert_grad(items):
        in_rows, grad_rows, up_pair, down_pair = items
        total = jnp.zeros((in_rows.shape[0], D), jnp.float32)
        for half in range(2):
            pre = jnp.zeros((in_rows.shape[0], half_ff), jnp.float32)
            hidden_grad = jnp.zeros((in_rows.shape[0], half_ff), jnp.float32)
            for part in range(N_EXP):
                lower = part * group
                upper = lower + group
                term = jnp.dot(in_rows[:, lower:upper], up_pair[half, lower:upper, :], preferred_element_type=jnp.float32)
                pre = pre + lax.optimization_barrier(term.astype(jnp.bfloat16)).astype(jnp.float32)
                other = lax.dot_general(grad_rows[:, lower:upper], down_pair[half, :, lower:upper], (((1,), (1,)), ((), ())), preferred_element_type=jnp.float32)
                hidden_grad = hidden_grad + lax.optimization_barrier(other.astype(jnp.bfloat16)).astype(jnp.float32)
            slope = (hidden_grad * silu_slope(pre)).astype(jnp.bfloat16)
            back = lax.dot_general(slope, up_pair[half], (((1,), (1,)), ((), ())), preferred_element_type=jnp.float32)
            total = total + lax.optimization_barrier(back.astype(jnp.bfloat16)).astype(jnp.float32)
        return total
    expert_out = lax.map(expert_grad, (gather_rows(attn_out), gather_rows(out_grad), up_weight.reshape(EXPERTS, 2, D, half_ff), down_weight.reshape(EXPERTS, 2, half_ff, D)))
    expert_out = expert_out.reshape(EXPERTS, blocks, CAP, D).transpose(1, 0, 2, 3).reshape(blocks, EXPERTS * CAP, D)
    moe_grad = jnp.einsum('bsl,bsd->bld', weigh, expert_out, precision=HIGHEST).reshape(TOKENS, D)
    grad_out = (out_grad.astype(jnp.float32) + moe_grad).astype(jnp.bfloat16)

    def backward_step(state, items):
        query_blk, key_blk, value_blk, grad_blk, ahead = items
        query_wide = query_blk.astype(jnp.float32)
        key_wide = key_blk.astype(jnp.float32)
        value_wide = value_blk.astype(jnp.float32)
        grad_wide = grad_blk.astype(jnp.float32)
        scores = jnp.einsum('ihd,jhd->hij', query_wide, key_wide)
        weights = (scale * scores * within).astype(jnp.bfloat16).astype(jnp.float32)
        dscores = jnp.einsum('ihd,jhd->hij', grad_wide, value_wide)
        dweights = (scale * dscores * within).astype(jnp.bfloat16).astype(jnp.float32)
        query_g = jnp.einsum('hij,jhd->ihd', dweights, key_wide) + scale * start_pow[:, :, None] * jnp.einsum('ihe,hde->ihd', grad_wide, ahead, precision=HIGHEST)
        key_g = jnp.einsum('hij,ihd->jhd', dweights, query_wide) + scale * last_pow[:, :, None] * jnp.einsum('jhe,hde->jhd', value_wide, state, precision=HIGHEST)
        value_g = jnp.einsum('hij,ihd->jhd', weights, grad_wide) + scale * last_pow[:, :, None] * jnp.einsum('jhd,hde->jhe', key_wide, state, precision=HIGHEST)
        local = jnp.einsum('ihd,ihe->hde', query_wide * next_pow[:, :, None], grad_wide, precision=HIGHEST)
        outs = (query_g.astype(jnp.bfloat16), key_g.astype(jnp.bfloat16), value_g.astype(jnp.bfloat16))
        return (whole_pow[:, None, None] * state + local, outs)
    unused_end, (query_grad, key_grad, value_grad) = lax.scan(backward_step, zero_state, (blocked(queries), blocked(keys), blocked(values), blocked(grad_out), entering), reverse=True)
    return (query_grad.reshape(TOKENS, D), key_grad.reshape(TOKENS, D), value_grad.reshape(TOKENS, D))
```

```python
import functools
import jax
import jax.numpy as jnp
from jax import lax
from jax.experimental import pallas as pl
from jax.experimental.pallas import tpu as pltpu
from jax.sharding import PartitionSpec as P

DH = 128


HIGHEST = lax.Precision.HIGHEST


def silu_slope(value):
    sigma = jax.nn.sigmoid(value)
    return sigma * (1.0 + value * (1.0 - sigma))


def decay_tables(rates, block_len):
    offsets = jnp.arange(block_len).astype(jnp.float32)
    distance = offsets[:, None] - offsets[None, :]
    within = jnp.where(
        distance[None] >= 0.0,
        jnp.exp(-rates[:, None, None] * jnp.maximum(distance, 0.0)[None]),
        0.0,
    )
    start_pow = jnp.exp(-rates[None, :] * offsets[:, None])
    end_pow = jnp.exp(-rates[None, :] * (block_len - offsets)[:, None])
    last_pow = jnp.exp(-rates[None, :] * (block_len - 1.0 - offsets)[:, None])
    next_pow = jnp.exp(-rates[None, :] * (offsets + 1.0)[:, None])
    whole_pow = jnp.exp(-rates * block_len)
    return (within, start_pow, end_pow, last_pow, next_pow, whole_pow)


def slot_tables(route_block, gate_block, experts, capacity):
    flat = route_block.reshape(-1)
    hits = (flat[:, None] == jnp.arange(experts, dtype=jnp.int32)[None, :]).astype(jnp.int32)
    before = jnp.cumsum(hits, axis=0) - hits
    placed = jnp.sum(before * hits, axis=1)
    target = flat * capacity + placed
    match = (target[None, :] == jnp.arange(experts * capacity, dtype=jnp.int32)[:, None]).astype(
        jnp.float32
    )
    match = match.reshape(experts * capacity, route_block.shape[0], route_block.shape[1])
    return (jnp.sum(match, axis=2), jnp.sum(match * gate_block[None], axis=2))


MESH = pl.DeviceIdType.MESH


def scan_kernel(reverse, rates_ref, local_ref, out_ref, got, made, send_a, recv_a, send_b, recv_b):
    n = local_ref.shape[0]
    rows = local_ref.shape[1]
    me = lax.axis_index("ctx")
    barrier = pltpu.get_barrier_semaphore()

    def greet(k, carry):
        pl.semaphore_signal(barrier, inc=1, device_id={"ctx": lax.rem(me + k, n)}, device_id_type=MESH)
        return carry

    lax.fori_loop(1, n, greet, 0)
    got[me] = local_ref[me]
    pl.semaphore_wait(barrier, n - 1)

    def first(k):
        peer = lax.rem(me + k, n)
        return pltpu.make_async_remote_copy(
            src_ref=local_ref.at[peer],
            dst_ref=got.at[me],
            send_sem=send_a.at[k],
            recv_sem=recv_a.at[k],
            device_id={"ctx": peer},
            device_id_type=MESH,
        )

    def second(k):
        peer = lax.rem(me + k, n)
        return pltpu.make_async_remote_copy(
            src_ref=made.at[peer],
            dst_ref=out_ref.at[me],
            send_sem=send_b.at[k],
            recv_sem=recv_b.at[k],
            device_id={"ctx": peer},
            device_id_type=MESH,
        )

    def loop(action):
        def body(k, carry):
            action(k)
            return carry

        lax.fori_loop(1, n, body, 0)

    loop(lambda k: first(k).start())
    row = lax.broadcasted_iota(jnp.int32, (rows, DH), 0) + me * rows
    rate = jnp.zeros((rows, DH), jnp.float32)
    for head in range(rates_ref.shape[0]):
        inside = (row >= head * DH) & (row < (head + 1) * DH)
        rate = jnp.where(inside, rates_ref[head], rate)
    factor = jnp.exp(-rate * float(DH))
    loop(lambda k: first(k).wait_recv())

    def step(i, total):
        c = n - 1 - i if reverse else i
        made[c] = total.astype(made.dtype)
        return factor * total + got[c].astype(jnp.float32)

    lax.fori_loop(0, n, step, jnp.zeros((rows, DH), jnp.float32))
    loop(lambda k: second(k).start())
    out_ref[me] = made[me]
    loop(lambda k: second(k).wait_recv())
    loop(lambda k: first(k).wait_send())
    loop(lambda k: second(k).wait_send())


def states(rates, local, reverse):
    heads = local.shape[0]
    n = lax.axis_size("ctx")
    rows = heads * DH // n
    pieces = local.astype(jnp.bfloat16).reshape(n, rows, DH)
    out = pl.pallas_call(
        functools.partial(scan_kernel, reverse),
        out_shape=jax.ShapeDtypeStruct(pieces.shape, jnp.bfloat16),
        in_specs=[pl.BlockSpec(memory_space=pltpu.SMEM), pl.BlockSpec(memory_space=pltpu.VMEM)],
        out_specs=pl.BlockSpec(memory_space=pltpu.VMEM),
        scratch_shapes=[pltpu.VMEM(pieces.shape, jnp.bfloat16)] * 2 + [pltpu.SemaphoreType.DMA((n,))] * 4,
        compiler_params=pltpu.CompilerParams(collective_id=1 if reverse else 0, has_side_effects=True),
    )(rates, pieces)
    return out.reshape(heads, DH, DH).astype(jnp.float32)


def contract_last(left, right):
    return lax.dot_general(
        left, right, (((1,), (1,)), ((), ())), preferred_element_type=jnp.float32
    )


def on_device(
    queries, keys, values, out_grad, up_weight, down_weight, decay_rates, routes, gate_weights
):
    block_len = queries.shape[0]
    group = queries.shape[1]
    heads = group // DH
    scale = 1.0 / DH
    within, start_pow, end_pow, last_pow, next_pow, whole_pow = decay_tables(decay_rates, block_len)
    query_heads = queries.reshape(block_len, heads, DH)
    key_heads = keys.reshape(block_len, heads, DH)
    value_heads = values.reshape(block_len, heads, DH)
    query_wide = query_heads.astype(jnp.float32)
    key_wide = key_heads.astype(jnp.float32)
    value_wide = value_heads.astype(jnp.float32)
    scores = jnp.einsum("ihd,jhd->hij", query_heads, key_heads, preferred_element_type=jnp.float32)
    weights = (scale * scores * within).astype(jnp.bfloat16)
    intra = jnp.einsum("hij,jhd->ihd", weights, value_heads, preferred_element_type=jnp.float32)
    key_local = jnp.einsum(
        "ihd,ihe->hde", key_wide * end_pow[:, :, None], value_wide, precision=HIGHEST
    )
    entering = states(decay_rates, key_local, False)
    inter = (
        scale
        * start_pow[:, :, None]
        * jnp.einsum("ihd,hde->ihe", query_wide, entering, precision=HIGHEST)
    )
    attn_out = (intra + inter).astype(jnp.bfloat16).reshape(block_len, group)
    experts = lax.axis_size("ctx") // 2
    capacity = block_len * 9 // (4 * experts)
    choose, weigh = slot_tables(routes, gate_weights, experts, capacity)
    choose_half = choose.astype(jnp.bfloat16)
    send_in = jnp.dot(choose_half, attn_out, preferred_element_type=jnp.float32).astype(
        jnp.bfloat16
    )
    send_grad = jnp.dot(choose_half, out_grad, preferred_element_type=jnp.float32).astype(
        jnp.bfloat16
    )

    def doubled(array):
        spread = jnp.broadcast_to(
            array.reshape(experts, 1, capacity, group), (experts, 2, capacity, group)
        )
        return spread.reshape(2 * experts, capacity, group)

    got_in, got_grad = (
        lax.all_to_all(doubled(send_in), "ctx", split_axis=0, concat_axis=0, tiled=True),
        lax.all_to_all(doubled(send_grad), "ctx", split_axis=0, concat_axis=0, tiled=True),
    )
    in_rows = got_in.reshape(-1, group)
    grad_rows = got_grad.reshape(-1, group)
    up_local = up_weight[0]
    down_local = down_weight[0]
    pre_part = jnp.dot(in_rows, up_local, preferred_element_type=jnp.float32)
    grad_part = contract_last(grad_rows, down_local)
    pre, hidden_grad = (
        lax.psum(pre_part.astype(jnp.bfloat16), "exp").astype(jnp.float32),
        lax.psum(grad_part.astype(jnp.bfloat16), "exp").astype(jnp.float32),
    )
    slope = (hidden_grad * silu_slope(pre)).astype(jnp.bfloat16)
    back = contract_last(slope, up_local)
    back_half = back.astype(jnp.bfloat16).reshape(2 * experts, capacity, group)
    home = lax.all_to_all(back_half, "ctx", split_axis=0, concat_axis=0, tiled=True)
    summed = jnp.sum(home.astype(jnp.float32).reshape(experts, 2, capacity, group), axis=1)
    summed = summed.reshape(experts * capacity, group)
    moe_grad = lax.dot_general(
        weigh,
        summed,
        (((0,), (0,)), ((), ())),
        precision=HIGHEST,
        preferred_element_type=jnp.float32,
    )
    grad_out = (out_grad.astype(jnp.float32) + moe_grad).astype(jnp.bfloat16)
    grad_heads = grad_out.reshape(block_len, heads, DH)
    grad_wide = grad_heads.astype(jnp.float32)
    query_local = jnp.einsum(
        "ihd,ihe->hde", query_wide * next_pow[:, :, None], grad_wide, precision=HIGHEST
    )
    leaving = states(decay_rates, query_local, True)
    dscores = jnp.einsum(
        "ihd,jhd->hij", grad_heads, value_heads, preferred_element_type=jnp.float32
    )
    dweights = (scale * dscores * within).astype(jnp.bfloat16)
    query_g = jnp.einsum("hij,jhd->ihd", dweights, key_heads, preferred_element_type=jnp.float32)
    query_g = query_g + scale * start_pow[:, :, None] * jnp.einsum(
        "ihe,hde->ihd", grad_wide, entering, precision=HIGHEST
    )
    key_g = jnp.einsum("hij,ihd->jhd", dweights, query_heads, preferred_element_type=jnp.float32)
    key_g = key_g + scale * last_pow[:, :, None] * jnp.einsum(
        "jhe,hde->jhd", value_wide, leaving, precision=HIGHEST
    )
    value_g = jnp.einsum("hij,ihd->jhd", weights, grad_heads, preferred_element_type=jnp.float32)
    value_g = value_g + scale * last_pow[:, :, None] * jnp.einsum(
        "jhd,hde->jhe", key_wide, leaving, precision=HIGHEST
    )
    return (
        query_g.astype(jnp.bfloat16).reshape(block_len, group),
        key_g.astype(jnp.bfloat16).reshape(block_len, group),
        value_g.astype(jnp.bfloat16).reshape(block_len, group),
    )


def solution(mesh):
    placed = (
        P("ctx", "exp"),
        P("ctx", "exp"),
        P("ctx", "exp"),
        P("ctx", "exp"),
        P("ctx", "exp", None),
        P("ctx", None, "exp"),
        P("exp"),
        P("ctx", None),
        P("ctx", None),
    )
    return jax.shard_map(
        on_device,
        mesh=mesh,
        in_specs=placed,
        out_specs=(P("ctx", "exp"), P("ctx", "exp"), P("ctx", "exp")),
        check_vma=False,
    )
```

```python
import jax
import jax.numpy as jnp
from jax import lax
from jax.experimental import pallas as pl
from jax.experimental.pallas import tpu as pltpu
from jax.sharding import PartitionSpec as P

DH = 128
MESH = pl.DeviceIdType.MESH
BF = jnp.bfloat16
F32 = jnp.float32
CHUNKS = (8, 8)
MAIN = 16
EXTRA = 2
QUARTERS = 4


def nn(left, right):
    return lax.dot_general(left, right, (((1,), (0,)), ((), ())), preferred_element_type=F32)


def nt(left, right):
    return lax.dot_general(left, right, (((1,), (1,)), ((), ())), preferred_element_type=F32)


def tn(left, right):
    return lax.dot_general(left, right, (((0,), (0,)), ((), ())), preferred_element_type=F32)


def iota(shape, dim):
    return lax.broadcasted_iota(jnp.int32, shape, dim)


def each(lower, upper, action):
    def body(i, carry):
        action(i)
        return carry

    lax.fori_loop(lower, upper, body, 0)


class Remote:
    def __init__(self, make):
        self.make = make

    def start(self, *index):
        self.make(*index).start()

    def arrived(self, *index):
        self.make(*index).wait_recv()

    def left(self, *index):
        self.make(*index).wait_send()


def layer_kernel(
    rates, routes, gates, queries, keys, values, out_grad, up_hbm, down_hbm,
    query_g, key_g, value_g,
    up, down, main_hot, extra_hot, send_main, send_extra, rows_in, extra_in, partial,
    turned, below, above, slope, back, crossed, final, home_extra_out, home, home_extra,
    weights, intra, attn, local, got, made, entering, local_b, got_b, made_b, leaving, grad_out,
    key_part, value_part,
    weight_sem, main_s, main_r, relay_s, relay_r, extra_s, extra_r, hop_s, hop_r,
    fore_s, fore_r, rear_s, rear_r, reduce_s, reduce_r, gather_s, gather_r, cross_s, cross_r,
    home_s, home_r, homex_s, homex_r,
):
    block = queries.shape[0]
    group = queries.shape[1]
    heads = group // DH
    hidden = up.shape[1]
    half = hidden // 2
    quarter = group // QUARTERS
    scale = 1.0 / DH
    ctx = lax.axis_size("ctx")
    chips = ctx // 2
    me = lax.axis_index("ctx")
    level = lax.axis_index("exp")
    chip = lax.div(me, 2)
    core = lax.rem(me, 2)
    partner = me + 1 - 2 * core
    nxt, opp, prv = (lax.rem(level + i, 4) for i in (1, 2, 3))

    barrier = pltpu.get_barrier_semaphore()
    each(1, ctx, lambda k: pl.semaphore_signal(
        barrier, inc=1, device_id={"ctx": lax.rem(me + k, ctx)}, device_id_type=MESH))
    for peer in (nxt, prv):
        pl.semaphore_signal(barrier, inc=1, device_id={"exp": peer}, device_id_type=MESH)
    load_down = pltpu.make_async_copy(down_hbm.at[0], down, weight_sem.at[0])
    load_up = pltpu.make_async_copy(up_hbm.at[0], up, weight_sem.at[1])
    load_down.start()
    load_up.start()

    spans, base, short, first = [], 0, 0, 0
    for number, n in enumerate(CHUNKS):
        tall = 8 * n + (MAIN if number == 0 else 0)
        spans.append((first, n, base, tall, short))
        first, base, short = first + n, base + 4 * tall, short + tall

    def block_row(number, owner_base, local_k):
        first_k, n, start, tall, _ = spans[number]
        each_owner = n // 2
        owner = owner_base + lax.div(local_k, each_owner)
        return pl.multiple_of(start + owner * tall + lax.rem(local_k, each_owner) * MAIN, MAIN)

    expert = iota((block, chips), 1)
    hits = [(routes[:, k : k + 1] == expert).astype(F32) for k in range(2)]
    earlier = (iota((block, block), 1) < iota((block, block), 0)).astype(BF)
    before = nn(earlier, (hits[0] + hits[1]).astype(BF))
    for k in range(2):
        placed = jnp.sum(before * hits[k], axis=1, keepdims=True).astype(jnp.int32)
        chosen = routes[:, k : k + 1]
        target = jnp.where(placed < MAIN, chosen * MAIN + placed, -1)
        main_hot[k] = (target == iota((block, chips * MAIN), 1)).astype(F32).astype(BF)
        spare = jnp.where(placed >= MAIN, chosen * 8 + placed - MAIN, -64)
        for q in range(QUARTERS):
            extra_hot[k, q] = (spare + EXTRA * q == iota((block, chips * 8), 1)).astype(F32).astype(BF)

    def gather(a, source):
        pick = main_hot[0] + main_hot[1]

        def columns(i):
            cols = pl.ds(pl.multiple_of(i * 256, 256), 256)
            send_main[a, :, cols] = tn(pick, source[:, cols]).astype(BF)

        each(0, group // 256, columns)
        total = jnp.zeros((chips * 8, quarter), F32)
        for q in range(QUARTERS):
            total += tn(extra_hot[0, q] + extra_hot[1, q], source[:, q * quarter : (q + 1) * quarter])
        send_extra[a] = total.astype(BF).reshape(chips, 8, quarter)

    def same_core(k):
        return lax.rem(chip + k, chips) * 2 + core

    def dispatch(a, number):
        first_k = spans[number][0]

        def make(k):
            return pltpu.make_async_remote_copy(
                src_ref=send_main.at[a, pl.ds(pl.multiple_of(lax.rem(chip + k, chips) * MAIN, MAIN), MAIN), :],
                dst_ref=rows_in.at[a, pl.ds(block_row(number, 2 * core, k - first_k), MAIN), :],
                send_sem=main_s.at[a, k], recv_sem=main_r.at[a, k],
                device_id={"ctx": same_core(k)}, device_id_type=MESH)

        return Remote(make)

    def relay(a, number, side):
        first_k = spans[number][0]

        def make(k):
            rows = rows_in.at[a, pl.ds(block_row(number, 2 * side, k - first_k), MAIN), :]
            return pltpu.make_async_remote_copy(
                src_ref=rows, dst_ref=rows, send_sem=relay_s.at[a, k], recv_sem=relay_r.at[a, k],
                device_id={"ctx": partner}, device_id_type=MESH)

        return Remote(make)

    def dispatch_extra(a):
        def make(k):
            return pltpu.make_async_remote_copy(
                src_ref=send_extra.at[a, lax.rem(chip + k, chips)], dst_ref=extra_in.at[a, core * chips + k],
                send_sem=extra_s.at[a, k], recv_sem=extra_r.at[a, k],
                device_id={"ctx": same_core(k)}, device_id_type=MESH)

        return Remote(make)

    def relay_extra(a, side):
        def make(k):
            rows = extra_in.at[a, side * chips + k]
            return pltpu.make_async_remote_copy(
                src_ref=rows, dst_ref=rows, send_sem=hop_s.at[a, k], recv_sem=hop_r.at[a, k],
                device_id={"ctx": partner}, device_id_type=MESH)

        return Remote(make)

    def send_rows(a, number):
        first_k, n = spans[number][:2]
        if number == 0:
            extra = dispatch_extra(a)
            each(1, chips, extra.start)
            extra_in[a, core * chips] = send_extra[a, chip]
            relay_extra(a, core).start(0)
            mine = send_main[a, pl.ds(pl.multiple_of(chip * MAIN, MAIN), MAIN), :]
            rows_in[a, pl.ds(block_row(0, 2 * core, 0), MAIN), :] = mine
            relay(a, 0, core).start(0)
        each(max(first_k, 1), first_k + n, dispatch(a, number).start)

    def pass_on(a, number):
        first_k, n = spans[number][:2]
        if number == 0:
            arriving, onward = dispatch_extra(a), relay_extra(a, core)

            def step(k):
                arriving.arrived(k)
                onward.start(k)

            each(1, chips, step)
        arriving_rows, onward_rows = dispatch(a, number), relay(a, number, core)

        def row_step(k):
            arriving_rows.arrived(k)
            onward_rows.start(k)

        each(max(first_k, 1), first_k + n, row_step)

    def all_rows(a, number):
        first_k, n, start, tall, _ = spans[number]
        if number == 0:
            each(0, chips, relay_extra(a, 1 - core).arrived)
        each(first_k, first_k + n, relay(a, number, 1 - core).arrived)
        if number == 0:
            packed = extra_in[a].reshape(2 * chips * 8, quarter)
            count = 2 * chips * EXTRA
            row, col = iota((count, 2 * chips * 8), 0), iota((count, 2 * chips * 8), 1)
            origin = lax.div(row, 2) * 8 + lax.rem(row, 2)
            for q in range(QUARTERS):
                placed = nn((col == origin + EXTRA * q).astype(F32).astype(BF), packed).astype(BF)
                for owner in range(4):
                    at = start + owner * tall + tall - MAIN
                    rows_in[a, at : at + MAIN, q * quarter : (q + 1) * quarter] = placed[owner * MAIN : (owner + 1) * MAIN]

    def expert_in(a, number):
        start, tall = spans[number][2:4]

        def columns(i):
            at = pl.multiple_of(i * 256, 256)
            rows = rows_in[a, start : start + 4 * tall, :]
            if a == 0:
                product = nt(rows, down[pl.ds(at, 256), :])
            else:
                product = nn(rows, up[:, pl.ds(at, 256)])
            partial[a, start : start + 4 * tall, pl.ds(at, 256)] = product.astype(BF)

        each(0, hidden // 256, columns)

    low, high = pl.ds(0, half), pl.ds(half, half)

    def reducer(a, number, which):
        _, _, start, tall, rest = spans[number]

        def owned(by):
            return pl.ds(pl.multiple_of(start + by * tall, MAIN), tall)

        there = pl.ds(rest, tall)
        src, dst, peer = {
            "turn_up": ((owned(opp), low), (turned, 0, low), nxt),
            "turn_down": ((owned(opp), high), (turned, 0, high), prv),
            "own_up": ((owned(nxt), high), (below, 0, high), nxt),
            "own_down": ((owned(prv), low), (above, 0, low), prv),
            "sum_up": ((owned(nxt), low), (below, 0, low), nxt),
            "sum_down": ((owned(prv), high), (above, 0, high), prv),
        }[which]
        slot = ("turn_up", "turn_down", "own_up", "own_down", "sum_up", "sum_down").index(which)
        return pltpu.make_async_remote_copy(
            src_ref=partial.at[a, src[0], src[1]], dst_ref=dst[0].at[a, there, dst[2]],
            send_sem=reduce_s.at[a, number, slot], recv_sem=reduce_r.at[a, number, slot],
            device_id={"exp": peer}, device_id_type=MESH)

    def reduce_start(a, number):
        for which in ("turn_up", "turn_down", "own_up", "own_down"):
            reducer(a, number, which).start()

    def reduce_turn(a, number):
        _, _, start, tall, rest = spans[number]
        wide = half // 3
        for turn, onward, by, offset in (("turn_up", "sum_up", nxt, 0), ("turn_down", "sum_down", prv, half)):
            reducer(a, number, turn).wait_recv()
            rows = pl.ds(pl.multiple_of(start + by * tall, MAIN), tall)

            def columns(i):
                cols = pl.ds(pl.multiple_of(offset + i * wide, 128), wide)
                mine = partial[a, rows, cols].astype(F32) + turned[a, rest : rest + tall, cols].astype(F32)
                partial[a, rows, cols] = mine.astype(BF)

            each(0, 3, columns)
            reducer(a, number, onward).start()

    def finish(number):
        _, _, start, tall, rest = spans[number]
        for a in range(2):
            for which in ("own_up", "own_down", "sum_up", "sum_down"):
                reducer(a, number, which).wait_recv()
        rows = pl.ds(pl.multiple_of(start + level * tall, MAIN), tall)
        there = pl.ds(rest, tall)

        def columns(i):
            cols = pl.ds(pl.multiple_of(i * 128, 128), 128)

            def total(a):
                return (partial[a, rows, cols].astype(F32) + below[a, there, cols].astype(F32)
                        + above[a, there, cols].astype(F32))

            pre = total(1)
            sigma = jax.nn.sigmoid(pre)
            slope[rows, cols] = (total(0) * (sigma * (1.0 + pre * (1.0 - sigma)))).astype(BF)

        each(0, hidden // 128, columns)
        for which in ("up_low", "down_high", "up_high", "down_low"):
            spread(number, which).start()

    def spread(number, which):
        _, _, start, tall, _ = spans[number]

        def owned(by):
            return pl.ds(pl.multiple_of(start + by * tall, MAIN), tall)

        owner, cols, peer = {
            "up_low": (level, low, nxt),
            "up_high": (level, high, nxt),
            "down_high": (level, high, prv),
            "down_low": (level, low, prv),
            "on_up": (prv, low, nxt),
            "on_down": (nxt, high, prv),
        }[which]
        slot = ("up_low", "up_high", "down_high", "down_low", "on_up", "on_down").index(which)
        rows = slope.at[owned(owner), cols]
        return pltpu.make_async_remote_copy(
            src_ref=rows, dst_ref=rows,
            send_sem=gather_s.at[number, slot], recv_sem=gather_r.at[number, slot],
            device_id={"exp": peer}, device_id_type=MESH)

    def spread_on(number):
        spread(number, "up_low").wait_recv()
        spread(number, "on_up").start()
        spread(number, "down_high").wait_recv()
        spread(number, "on_down").start()

    def spread_done(number):
        for which in ("up_high", "down_low", "on_up", "on_down"):
            spread(number, which).wait_recv()

    def cross(number, side, piece):
        _, _, start, tall, rest = spans[number]
        cols = pl.ds(piece * (group // 2), group // 2)
        return pltpu.make_async_remote_copy(
            src_ref=back.at[pl.ds(pl.multiple_of(start + side * 2 * tall, MAIN), 2 * tall), cols],
            dst_ref=crossed.at[pl.ds(2 * rest, 2 * tall), cols],
            send_sem=cross_s.at[number, piece], recv_sem=cross_r.at[number, piece],
            device_id={"ctx": partner}, device_id_type=MESH)

    def expert_back(number):
        _, _, start, tall, _ = spans[number]

        def columns(i):
            at = pl.multiple_of(i * 256, 256)
            product = nt(slope[start : start + 4 * tall, :], up[pl.ds(at, 256), :])
            back[start : start + 4 * tall, pl.ds(at, 256)] = product.astype(BF)

        for piece in range(2):
            each(piece * 3, piece * 3 + 3, columns)
            cross(number, 1 - core, piece).start()

    def go_home(number):
        first_k, n, start, tall, rest = spans[number]

        def make(k):
            local_k = k - first_k
            row = 2 * rest + lax.div(local_k, n // 2) * tall + lax.rem(local_k, n // 2) * MAIN
            return pltpu.make_async_remote_copy(
                src_ref=final.at[pl.ds(pl.multiple_of(row, MAIN), MAIN), :],
                dst_ref=home.at[pl.ds(pl.multiple_of(chip * MAIN, MAIN), MAIN), :],
                send_sem=home_s.at[k], recv_sem=home_r.at[k],
                device_id={"ctx": same_core(chips - k)}, device_id_type=MESH)

        return Remote(make)

    def extra_home():
        def make(k):
            return pltpu.make_async_remote_copy(
                src_ref=home_extra_out.at[k], dst_ref=home_extra.at[chip],
                send_sem=homex_s.at[k], recv_sem=homex_r.at[k],
                device_id={"ctx": same_core(chips - k)}, device_id_type=MESH)

        return Remote(make)

    def return_rows(number):
        first_k, n, start, tall, rest = spans[number]
        own = pl.multiple_of(start + core * 2 * tall, MAIN)
        for piece in range(2):
            cross(number, core, piece).wait_recv()

            def columns(i):
                cols = pl.ds(pl.multiple_of(i * 256, 256), 256)
                mine = back[pl.ds(own, 2 * tall), cols].astype(F32)
                mine += crossed[2 * rest : 2 * rest + 2 * tall, cols].astype(F32)
                final[2 * rest : 2 * rest + 2 * tall, cols] = mine.astype(BF)

            each(piece * 3, piece * 3 + 3, columns)
        if number == 0:
            count = chips * EXTRA
            row, col = iota((chips * 8, count), 1), iota((chips * 8, count), 0)
            origin = lax.div(row, 2) * 8 + lax.rem(row, 2)
            total = jnp.zeros((chips * 8, quarter), F32)
            for q in range(QUARTERS):
                cols = slice(q * quarter, (q + 1) * quarter)
                spare = jnp.concatenate(
                    [final[2 * rest + (o + 1) * tall - MAIN : 2 * rest + (o + 1) * tall, cols] for o in range(2)], axis=0)
                total += nn((col == origin + EXTRA * q).astype(F32).astype(BF), spare)
            home_extra_out[...] = total.astype(BF).reshape(chips, 8, quarter)
            each(1, chips, extra_home().start)
            home_extra[chip] = home_extra_out[0]
            home[pl.ds(pl.multiple_of(chip * MAIN, MAIN), MAIN), :] = final[2 * rest : 2 * rest + MAIN, :]
        each(max(first_k, 1), first_k + n, go_home(number).start)

    pieces = local.shape[0] // ctx

    def piece_rows(number):
        return pl.ds(pl.multiple_of(number * pieces, MAIN), pieces)

    def scan_out(source, target, sems):
        def make(k):
            peer = lax.rem(me + k, ctx)
            return pltpu.make_async_remote_copy(
                src_ref=source.at[piece_rows(peer), :], dst_ref=target.at[piece_rows(me), :],
                send_sem=sems[0].at[sems[2], k], recv_sem=sems[1].at[sems[2], k],
                device_id={"ctx": peer}, device_id_type=MESH)

        return Remote(make)

    def scan_local(arrived, prefixes, reverse):
        row = iota((pieces, DH), 0) + me * pieces
        rate = jnp.zeros((pieces, DH), F32)
        for h in range(heads):
            rate = jnp.where((row >= h * DH) & (row < (h + 1) * DH), rates[h], rate)
        factor = jnp.exp(-rate * float(block))

        def step(i, total):
            at = piece_rows(ctx - 1 - i if reverse else i)
            prefixes[at, :] = total.astype(BF)
            return factor * total + arrived[at, :].astype(F32)

        lax.fori_loop(0, ctx, step, jnp.zeros((pieces, DH), F32))

    fore, fore_back = (local, got, (fore_s, fore_r, 0)), (made, entering, (fore_s, fore_r, 1))
    rear, rear_back = (local_b, got_b, (rear_s, rear_r, 0)), (made_b, leaving, (rear_s, rear_r, 1))
    place = iota((block, DH), 0).astype(F32)

    def head_cols(h):
        return slice(h * DH, (h + 1) * DH)

    def scan_first(path):
        each(1, ctx, scan_out(*path).start)
        path[1][piece_rows(me), :] = path[0][piece_rows(me), :]

    def scan_second(path, path_back, reverse):
        each(1, ctx, scan_out(*path).arrived)
        scan_local(path[1], path_back[0], reverse)
        each(1, ctx, scan_out(*path_back).start)
        path_back[1][piece_rows(me), :] = path_back[0][piece_rows(me), :]

    def within(h):
        distance = (iota((block, block), 0) - iota((block, block), 1)).astype(F32)
        return jnp.where(distance >= 0.0, jnp.exp(-rates[h] * jnp.maximum(distance, 0.0)), 0.0)

    gather(0, out_grad)
    pl.semaphore_wait(barrier, ctx - 1 + 2)
    send_rows(0, 0)
    for h in range(heads):
        faded = (keys[:, head_cols(h)].astype(F32) * jnp.exp(-rates[h] * (float(block) - place))).astype(BF)
        local[h * DH : (h + 1) * DH, :] = tn(faded, values[:, head_cols(h)]).astype(BF)
    scan_first(fore)
    for number in range(1, len(CHUNKS)):
        send_rows(0, number)
    for h in range(heads):
        score = nt(queries[:, head_cols(h)], keys[:, head_cols(h)])
        weight = (scale * score * within(h)).astype(BF)
        weights[h] = weight
        intra[:, head_cols(h)] = nn(weight, values[:, head_cols(h)])
    pass_on(0, 0)
    scan_second(fore, fore_back, False)
    all_rows(0, 0)
    load_down.wait()
    expert_in(0, 0)
    reduce_start(0, 0)
    for number in range(1, len(CHUNKS)):
        pass_on(0, number)
    each(1, ctx, scan_out(*fore_back).arrived)
    for h in range(heads):
        across = nn(queries[:, head_cols(h)], entering[h * DH : (h + 1) * DH, :])
        total = intra[:, head_cols(h)] + scale * jnp.exp(-rates[h] * place) * across
        attn[:, head_cols(h)] = total.astype(BF)
    gather(1, attn)
    for number in range(len(CHUNKS)):
        send_rows(1, number)
    for number in range(1, len(CHUNKS)):
        all_rows(0, number)
        expert_in(0, number)
        reduce_start(0, number)
        reduce_turn(0, number - 1)
    pass_on(1, 0)
    reduce_turn(0, len(CHUNKS) - 1)
    all_rows(1, 0)
    load_up.wait()
    expert_in(1, 0)
    reduce_start(1, 0)
    for number in range(1, len(CHUNKS)):
        pass_on(1, number)
        reduce_turn(1, number - 1)
        all_rows(1, number)
        expert_in(1, number)
        reduce_start(1, number)
        finish(number - 1)
        reduce_turn(1, number)
        spread_on(number - 1)
    finish(len(CHUNKS) - 1)
    for number in range(len(CHUNKS)):
        spread_done(number)
        expert_back(number)
        if number + 1 < len(CHUNKS):
            spread_on(number + 1)
        return_rows(number)

    each(1, chips, extra_home().arrived)
    for number, (first_k, n, *_) in enumerate(spans):
        each(max(first_k, 1), first_k + n, go_home(number).arrived)
    for q in range(QUARTERS):
        cols = slice(q * quarter, (q + 1) * quarter)
        total = out_grad[:, cols].astype(F32)
        for k in range(2):
            mine = nn(main_hot[k], home[:, cols])
            mine += nn(extra_hot[k, q], home_extra[...].reshape(chips * 8, quarter))
            total += gates[:, k : k + 1] * mine
        grad_out[:, cols] = total.astype(BF)
    for h in range(heads):
        faded = (queries[:, head_cols(h)].astype(F32) * jnp.exp(-rates[h] * (place + 1.0))).astype(BF)
        local_b[h * DH : (h + 1) * DH, :] = tn(faded, grad_out[:, head_cols(h)]).astype(BF)
    scan_first(rear)
    for h in range(heads):
        cols = head_cols(h)
        grad = grad_out[:, cols]
        dweight = (scale * nt(grad, values[:, cols]) * within(h)).astype(BF)
        across = nt(grad, entering[h * DH : (h + 1) * DH, :])
        query_g[:, cols] = (nn(dweight, keys[:, cols]) + scale * jnp.exp(-rates[h] * place) * across).astype(BF)
        key_part[:, cols] = tn(dweight, queries[:, cols])
        value_part[:, cols] = tn(weights[h], grad)
    scan_second(rear, rear_back, True)
    each(1, ctx, scan_out(*rear_back).arrived)
    for h in range(heads):
        cols = head_cols(h)
        state = leaving[h * DH : (h + 1) * DH, :]
        fade = scale * jnp.exp(-rates[h] * (float(block) - 1.0 - place))
        key_g[:, cols] = (key_part[:, cols] + fade * nt(values[:, cols], state)).astype(BF)
        value_g[:, cols] = (value_part[:, cols] + fade * nn(keys[:, cols], state)).astype(BF)

    for path in (fore, fore_back, rear, rear_back):
        each(1, ctx, scan_out(*path).left)
    for a in range(2):
        each(1, chips, dispatch_extra(a).left)
        each(0, chips, relay_extra(a, core).left)
        for number, (first_k, n, *_) in enumerate(spans):
            each(max(first_k, 1), first_k + n, dispatch(a, number).left)
            each(first_k, first_k + n, relay(a, number, core).left)
            for which in ("turn_up", "turn_down", "own_up", "own_down", "sum_up", "sum_down"):
                reducer(a, number, which).wait_send()
    each(1, chips, extra_home().left)
    for number, (first_k, n, *_) in enumerate(spans):
        each(max(first_k, 1), first_k + n, go_home(number).left)
        for piece in range(2):
            cross(number, 1 - core, piece).wait_send()
        for which in ("up_low", "up_high", "down_high", "down_low", "on_up", "on_down"):
            spread(number, which).wait_send()


def on_device(
    queries, keys, values, out_grad, up_weight, down_weight, decay_rates, routes, gate_weights
):
    block, group = queries.shape
    heads = group // DH
    hidden = up_weight.shape[2]
    ctx = lax.axis_size("ctx")
    chips = ctx // 2
    slots = chips * MAIN
    total = 2 * chips * (MAIN + EXTRA)
    quarter = group // QUARTERS
    count = len(CHUNKS)
    state = (heads * DH, DH)
    dma = pltpu.SemaphoreType.DMA
    whole = pl.BlockSpec(memory_space=pltpu.VMEM)
    raw = pl.BlockSpec(memory_space=pl.ANY)
    out = jax.ShapeDtypeStruct((block, group), BF)
    return pl.pallas_call(
        layer_kernel,
        out_shape=(out, out, out),
        in_specs=[pl.BlockSpec(memory_space=pltpu.SMEM)] + [whole] * 6 + [raw] * 2,
        out_specs=(whole, whole, whole),
        scratch_shapes=[
            pltpu.VMEM((group, hidden), BF),
            pltpu.VMEM((hidden, group), BF),
            pltpu.VMEM((2, block, slots), BF),
            pltpu.VMEM((2, QUARTERS, block, chips * 8), BF),
            pltpu.VMEM((2, slots, group), BF),
            pltpu.VMEM((2, chips, 8, quarter), BF),
            pltpu.VMEM((2, total, group), BF),
            pltpu.VMEM((2, 2 * chips, 8, quarter), BF),
            pltpu.VMEM((2, total, hidden), BF),
            pltpu.VMEM((2, total // 4, hidden), BF),
            pltpu.VMEM((2, total // 4, hidden), BF),
            pltpu.VMEM((2, total // 4, hidden), BF),
            pltpu.VMEM((total, hidden), BF),
            pltpu.VMEM((total, group), BF),
            pltpu.VMEM((total // 2, group), BF),
            pltpu.VMEM((total // 2, group), BF),
            pltpu.VMEM((chips, 8, quarter), BF),
            pltpu.VMEM((slots, group), BF),
            pltpu.VMEM((chips, 8, quarter), BF),
            pltpu.VMEM((heads, block, block), BF),
            pltpu.VMEM((block, group), F32),
            pltpu.VMEM((block, group), BF),
        ]
        + [pltpu.VMEM(state, BF)] * 8
        + [
            pltpu.VMEM((block, group), BF),
            pltpu.VMEM((block, group), F32),
            pltpu.VMEM((block, group), F32),
            dma((2,)),
        ]
        + [dma((2, chips))] * 8
        + [dma((2, ctx))] * 4
        + [dma((2, count, 6))] * 2
        + [dma((count, 6))] * 2
        + [dma((count, 2))] * 2
        + [dma((chips,))] * 4,
        compiler_params=pltpu.CompilerParams(
            collective_id=0, has_side_effects=True, vmem_limit_bytes=67043328
        ),
    )(decay_rates, routes, gate_weights, queries, keys, values, out_grad, up_weight, down_weight)


def solution(mesh):
    placed = (
        P("ctx", "exp"),
        P("ctx", "exp"),
        P("ctx", "exp"),
        P("ctx", "exp"),
        P("ctx", "exp", None),
        P("ctx", None, "exp"),
        P("exp"),
        P("ctx", None),
        P("ctx", None),
    )
    return jax.shard_map(
        on_device,
        mesh=mesh,
        in_specs=placed,
        out_specs=(P("ctx", "exp"), P("ctx", "exp"), P("ctx", "exp")),
        check_vma=False,
    )
```

```python
import jax
import jax.numpy as jnp
from jax import lax
from jax.experimental import pallas as pl
from jax.experimental.pallas import tpu as pltpu
from jax.sharding import PartitionSpec as P

DH = 128
MESH = pl.DeviceIdType.MESH
BF = jnp.bfloat16
F32 = jnp.float32
MID, FAR, NEAR = 0, 1, 2
CHUNKS = (6, 6, 4)
OFFSETS = (
    (3, 0), (1, 1), (1, 3), (3, 1), (3, 3), (0, 2),
    (2, 0), (1, 2), (3, 2), (2, 1), (2, 3), (2, 2),
    (0, 0), (0, 1), (0, 3), (1, 0),
)
OWN = OFFSETS.index((0, 0))
EXTRAS = FAR
MAIN = 16
EXTRA = 2
QUARTERS = 4


def nn(left, right):
    return lax.dot_general(left, right, (((1,), (0,)), ((), ())), preferred_element_type=F32)


def nt(left, right):
    return lax.dot_general(left, right, (((1,), (1,)), ((), ())), preferred_element_type=F32)


def tn(left, right):
    return lax.dot_general(left, right, (((0,), (0,)), ((), ())), preferred_element_type=F32)


def iota(shape, dim):
    return lax.broadcasted_iota(jnp.int32, shape, dim)


def each(lower, upper, action):
    def body(i, carry):
        action(i)
        return carry

    lax.fori_loop(lower, upper, body, 0)


def layer_kernel(
    rates_hbm, routes_hbm, gates_hbm, queries_hbm, keys_hbm, values_hbm, out_grad_hbm, up_hbm, down_hbm,
    query_out, key_out, value_out,
    query_g, key_g, value_g, rates, route_rows, gate_rows, queries, keys, values, out_grad, gates,
    up, down, main_hot, extra_hot, send_main, send_extra, rows_in, extra_in, partial,
    turned, below, above, slope, back, crossed, final, home_extra_out, home, home_extra,
    weights, intra, attn, local, entering, local_b, leaving, swap, summed, got, made, prefix, onward,
    swap_b, summed_b, got_b, made_b, prefix_b, onward_b, grad_out,
    key_part, value_part, faded_keys,
    load_sem, out_sem, main_s, main_r, relay_s, relay_r, extra_s, extra_r, hop_s, hop_r,
    fore_s, fore_r, rear_s, rear_r, reduce_s, reduce_r, gather_s, gather_r, cross_s, cross_r,
    home_s, home_r, homex_s, homex_r,
):
    block = queries.shape[0]
    group = queries.shape[1]
    heads = group // DH
    hidden = up.shape[1]
    half = hidden // 2
    quarter = group // QUARTERS
    scale = 1.0 / DH
    ctx = lax.axis_size("ctx")
    chips = ctx // 2
    me = lax.axis_index("ctx")
    level = lax.axis_index("exp")
    chip = lax.div(me, 2)
    core = lax.rem(me, 2)
    partner = me + 1 - 2 * core
    nxt, opp, prv = (lax.rem(level + i, 4) for i in (1, 2, 3))

    barrier = pltpu.get_barrier_semaphore()
    each(1, ctx, lambda k: pl.semaphore_signal(
        barrier, inc=1, device_id={"ctx": lax.rem(me + k, ctx)}, device_id_type=MESH))
    for peer in (nxt, prv):
        pl.semaphore_signal(barrier, inc=1, device_id={"exp": peer}, device_id_type=MESH)
    loads = [
        pltpu.make_async_copy(source, target, load_sem.at[i])
        for i, (source, target) in enumerate((
            (routes_hbm, route_rows), (out_grad_hbm, out_grad), (rates_hbm, rates), (keys_hbm, keys),
            (values_hbm, values), (queries_hbm, queries), (gates_hbm, gate_rows),
            (down_hbm.at[0], down), (up_hbm.at[0], up)))
    ]
    for load in loads:
        load.start()

    spans, base, short, first = [], 0, 0, 0
    for number, n in enumerate(CHUNKS):
        tall = 8 * n + (MAIN if number == EXTRAS else 0)
        spans.append((first, n, base, tall, short))
        first, base, short = first + n, base + 4 * tall, short + tall

    def block_row(k, side):
        number = sum(k >= first_k for first_k, *_ in spans) - 1
        first_k, n, start, tall, _ = spans[number]
        owner, place_in = divmod(k - first_k, n // 2)
        return pl.ds(pl.multiple_of(start + (2 * side + owner) * tall + place_in * MAIN, MAIN), MAIN)

    def chunk_slots(number):
        return range(spans[number][0], spans[number][0] + spans[number][1])

    loads[0].wait()
    diagonal = iota((block, block), 0) == iota((block, block), 1)

    def upright(row):
        return jnp.sum(jnp.where(diagonal, row, 0.0), axis=1, keepdims=True)

    routes = [upright(route_rows[k : k + 1, :].astype(F32)).astype(jnp.int32) for k in range(2)]
    expert = iota((block, chips), 1)
    hits = [(routes[k] == expert).astype(F32) for k in range(2)]
    earlier = (iota((block, block), 1) < iota((block, block), 0)).astype(BF)
    before = nn(earlier, (hits[0] + hits[1]).astype(BF))
    for k in range(2):
        placed = jnp.sum(before * hits[k], axis=1, keepdims=True).astype(jnp.int32)
        chosen = routes[k]
        target = jnp.where(placed < MAIN, chosen * MAIN + placed, -1)
        main_hot[k] = (target == iota((block, chips * MAIN), 1)).astype(F32).astype(BF)
        spare = jnp.where(placed >= MAIN, chosen * 8 + placed - MAIN, -64)
        for q in range(QUARTERS):
            extra_hot[k, q] = (spare + EXTRA * q == iota((block, chips * 8), 1)).astype(F32).astype(BF)

    def gather(a, source):
        pick = main_hot[0] + main_hot[1]

        def columns(i):
            cols = pl.ds(pl.multiple_of(i * 256, 256), 256)
            send_main[a, :, cols] = tn(pick, source[:, cols]).astype(BF)

        each(0, group // 256, columns)
        total = jnp.zeros((chips * 8, quarter), F32)
        for q in range(QUARTERS):
            total += tn(extra_hot[0, q] + extra_hot[1, q], source[:, q * quarter : (q + 1) * quarter])
        send_extra[a] = total.astype(BF).reshape(chips, 8, quarter)

    side_len = 4
    z, x = lax.div(chip, side_len), lax.rem(chip, side_len)

    def to_chip(k):
        dz, dx = OFFSETS[k]
        return lax.rem(z + dz, side_len) * side_len + lax.rem(x + dx, side_len)

    def from_chip(k):
        dz, dx = OFFSETS[k]
        return (lax.rem(z + side_len - dz, side_len) * side_len + lax.rem(x + side_len - dx, side_len)) * 2 + core

    def slot_rows(number):
        return pl.ds(pl.multiple_of(number * MAIN, MAIN), MAIN)

    def dispatch(a, k):
        return pltpu.make_async_remote_copy(
            src_ref=send_main.at[a, slot_rows(to_chip(k)), :], dst_ref=rows_in.at[a, block_row(k, core), :],
            send_sem=main_s.at[a], recv_sem=main_r.at[a, k],
            device_id={"ctx": to_chip(k) * 2 + core}, device_id_type=MESH)

    def relay(a, k, number):
        rows = rows_in.at[a, block_row(k, core), :]
        return pltpu.make_async_remote_copy(
            src_ref=rows, dst_ref=rows, send_sem=relay_s.at[a, number], recv_sem=relay_r.at[a, number],
            device_id={"ctx": partner}, device_id_type=MESH)

    def relay_all(a, number):
        rows = rows_in.at[a, pl.ds(spans[number][2], spans[number][1] * MAIN), :]
        return pltpu.make_async_remote_copy(
            src_ref=rows, dst_ref=rows, send_sem=relay_s.at[a, number], recv_sem=relay_r.at[a, number],
            device_id={"ctx": partner}, device_id_type=MESH)

    def dispatch_extra(a, k):
        return pltpu.make_async_remote_copy(
            src_ref=send_extra.at[a, to_chip(k)], dst_ref=extra_in.at[a, core * chips + k],
            send_sem=extra_s.at[a], recv_sem=extra_r.at[a],
            device_id={"ctx": to_chip(k) * 2 + core}, device_id_type=MESH)

    def dispatch_extra_all(a):
        return pltpu.make_async_remote_copy(
            src_ref=send_extra.at[a, pl.ds(0, chips - 1)], dst_ref=extra_in.at[a, pl.ds(0, chips - 1)],
            send_sem=extra_s.at[a], recv_sem=extra_r.at[a],
            device_id={"ctx": partner}, device_id_type=MESH)

    def relay_extra(a):
        rows = extra_in.at[a, pl.ds(core * chips, chips)]
        return pltpu.make_async_remote_copy(
            src_ref=rows, dst_ref=rows, send_sem=hop_s.at[a], recv_sem=hop_r.at[a],
            device_id={"ctx": partner}, device_id_type=MESH)

    def send_rows(a, number):
        if number == EXTRAS:
            for k in range(chips):
                if k != OWN:
                    dispatch_extra(a, k).start()
            extra_in[a, core * chips + OWN] = send_extra[a, chip]
        for k in chunk_slots(number):
            if k == OWN:
                rows_in[a, block_row(OWN, core), :] = send_main[a, slot_rows(chip), :]
                relay(a, OWN, number).start()
            else:
                dispatch(a, k).start()

    def pass_on(a, number):
        if number == EXTRAS:
            dispatch_extra_all(a).wait_recv()
            relay_extra(a).start()
        for k in chunk_slots(number):
            if k != OWN:
                dispatch(a, k).wait_recv()
                relay(a, k, number).start()

    def all_rows(a, number):
        _, _, start, tall, _ = spans[number]
        if number == EXTRAS:
            relay_extra(a).wait_recv()
            packed = extra_in[a].reshape(2 * chips * 8, quarter)
            count = 2 * chips * EXTRA
            row, col = iota((count, 2 * chips * 8), 0), iota((count, 2 * chips * 8), 1)
            origin = lax.div(row, 2) * 8 + lax.rem(row, 2)
            for q in range(QUARTERS):
                placed = nn((col == origin + EXTRA * q).astype(F32).astype(BF), packed).astype(BF)
                for owner in range(4):
                    at = start + owner * tall + tall - MAIN
                    rows_in[a, at : at + MAIN, q * quarter : (q + 1) * quarter] = placed[owner * MAIN : (owner + 1) * MAIN]
        relay_all(a, number).wait_recv()

    def expert_in(a, number):
        start, tall = spans[number][2:4]
        span = slice(start, start + 4 * tall)

        def block_of(at, wide):
            rows = rows_in[a, span, :]
            if a == 0:
                product = nt(rows, down[pl.ds(at, wide), :])
            else:
                product = nn(rows, up[:, pl.ds(at, wide)])
            partial[a, span, pl.ds(at, wide)] = product.astype(BF)

        for side, moves in enumerate((("turn_up", "own_down"), ("turn_down", "own_up"))):
            each(0, half // 256, lambda i: block_of(pl.multiple_of(side * half + i * 256, 128), 256))
            done = half // 256 * 256
            if done < half:
                block_of(side * half + done, half - done)
            for which in moves:
                reducer(a, number, which).start()

    low, high = pl.ds(0, half), pl.ds(half, half)

    def reducer(a, number, which):
        _, _, start, tall, rest = spans[number]

        def owned(by):
            return pl.ds(pl.multiple_of(start + by * tall, MAIN), tall)

        there = pl.ds(rest, tall)
        src, dst, peer = {
            "turn_up": ((owned(opp), low), (turned, 0, low), nxt),
            "turn_down": ((owned(opp), high), (turned, 0, high), prv),
            "own_up": ((owned(nxt), high), (below, 0, high), nxt),
            "own_down": ((owned(prv), low), (above, 0, low), prv),
            "sum_up": ((owned(nxt), low), (below, 0, low), nxt),
            "sum_down": ((owned(prv), high), (above, 0, high), prv),
        }[which]
        slot = ("turn_up", "turn_down", "own_up", "own_down", "sum_up", "sum_down").index(which)
        return pltpu.make_async_remote_copy(
            src_ref=partial.at[a, src[0], src[1]], dst_ref=dst[0].at[a, there, dst[2]],
            send_sem=reduce_s.at[a, number, slot], recv_sem=reduce_r.at[a, number, slot],
            device_id={"exp": peer}, device_id_type=MESH)

    def reduce_turn(a, number):
        _, _, start, tall, rest = spans[number]
        wide = half // 3
        for turn, onward, by, offset in (("turn_up", "sum_up", nxt, 0), ("turn_down", "sum_down", prv, half)):
            reducer(a, number, turn).wait_recv()
            rows = pl.ds(pl.multiple_of(start + by * tall, MAIN), tall)

            def columns(i):
                cols = pl.ds(pl.multiple_of(offset + i * wide, 128), wide)
                mine = partial[a, rows, cols].astype(F32) + turned[a, rest : rest + tall, cols].astype(F32)
                partial[a, rows, cols] = mine.astype(BF)

            each(0, 3, columns)
            reducer(a, number, onward).start()

    def finish(number):
        _, _, start, tall, rest = spans[number]
        for a in range(2):
            for which in ("own_up", "own_down", "sum_up", "sum_down"):
                reducer(a, number, which).wait_recv()
        rows = pl.ds(pl.multiple_of(start + level * tall, MAIN), tall)
        there = pl.ds(rest, tall)

        def columns(i):
            cols = pl.ds(pl.multiple_of(i * 384, 128), 384)

            def total(a):
                return (partial[a, rows, cols].astype(F32) + below[a, there, cols].astype(F32)
                        + above[a, there, cols].astype(F32))

            pre = total(1)
            sigma = jax.nn.sigmoid(pre)
            slope[rows, cols] = (total(0) * (sigma * (1.0 + pre * (1.0 - sigma)))).astype(BF)

        each(0, hidden // 384, columns)
        for which in ("up_low", "down_high", "up_high", "down_low"):
            spread(number, which).start()

    def spread(number, which):
        _, _, start, tall, _ = spans[number]

        def owned(by):
            return pl.ds(pl.multiple_of(start + by * tall, MAIN), tall)

        owner, cols, peer = {
            "up_low": (level, low, nxt),
            "up_high": (level, high, nxt),
            "down_high": (level, high, prv),
            "down_low": (level, low, prv),
            "on_up": (prv, low, nxt),
            "on_down": (nxt, high, prv),
        }[which]
        slot = ("up_low", "up_high", "down_high", "down_low", "on_up", "on_down").index(which)
        rows = slope.at[owned(owner), cols]
        return pltpu.make_async_remote_copy(
            src_ref=rows, dst_ref=rows,
            send_sem=gather_s.at[number, slot], recv_sem=gather_r.at[number, slot],
            device_id={"exp": peer}, device_id_type=MESH)

    def spread_on(number):
        spread(number, "up_low").wait_recv()
        spread(number, "on_up").start()
        spread(number, "down_high").wait_recv()
        spread(number, "on_down").start()

    def spread_done(number):
        for which in ("up_high", "down_low", "on_up", "on_down"):
            spread(number, which).wait_recv()

    def cross(number, side, piece):
        _, _, start, tall, rest = spans[number]
        cols = pl.ds(piece * (group // 2), group // 2)
        return pltpu.make_async_remote_copy(
            src_ref=back.at[pl.ds(pl.multiple_of(start + side * 2 * tall, MAIN), 2 * tall), cols],
            dst_ref=crossed.at[pl.ds(2 * rest, 2 * tall), cols],
            send_sem=cross_s.at[number, piece], recv_sem=cross_r.at[number, piece],
            device_id={"ctx": partner}, device_id_type=MESH)

    def expert_back(number, pieces_of=(0, 1)):
        _, _, start, tall, _ = spans[number]

        def columns(i):
            at = pl.multiple_of(i * 256, 256)
            product = nt(slope[start : start + 4 * tall, :], up[pl.ds(at, 256), :])
            back[start : start + 4 * tall, pl.ds(at, 256)] = product.astype(BF)

        for piece in pieces_of:
            each(piece * 3, piece * 3 + 3, columns)
            cross(number, 1 - core, piece).start()

    def go_home(k):
        number = sum(k >= first_k for first_k, *_ in spans) - 1
        first_k, n, _, tall, rest = spans[number]
        owner, place_in = divmod(k - first_k, n // 2)
        row = 2 * rest + owner * tall + place_in * MAIN
        return pltpu.make_async_remote_copy(
            src_ref=final.at[pl.ds(row, MAIN), :], dst_ref=home.at[slot_rows(chip), :],
            send_sem=home_s.at[0], recv_sem=home_r.at[0],
            device_id={"ctx": from_chip(k)}, device_id_type=MESH)

    def home_all():
        rows = pl.ds(0, (chips - 1) * MAIN)
        return pltpu.make_async_remote_copy(
            src_ref=final.at[rows, :], dst_ref=home.at[rows, :], send_sem=home_s.at[0], recv_sem=home_r.at[0],
            device_id={"ctx": partner}, device_id_type=MESH)

    def extra_home(k):
        return pltpu.make_async_remote_copy(
            src_ref=home_extra_out.at[k], dst_ref=home_extra.at[chip],
            send_sem=homex_s.at[0], recv_sem=homex_r.at[0],
            device_id={"ctx": from_chip(k)}, device_id_type=MESH)

    def extra_home_all():
        rows = pl.ds(0, chips - 1)
        return pltpu.make_async_remote_copy(
            src_ref=home_extra_out.at[rows], dst_ref=home_extra.at[rows],
            send_sem=homex_s.at[0], recv_sem=homex_r.at[0],
            device_id={"ctx": partner}, device_id_type=MESH)

    def return_rows(number):
        first_k, n, start, tall, rest = spans[number]
        own = pl.multiple_of(start + core * 2 * tall, MAIN)
        for piece in range(2):
            cross(number, core, piece).wait_recv()

            def columns(i):
                cols = pl.ds(pl.multiple_of(i * 256, 256), 256)
                mine = back[pl.ds(own, 2 * tall), cols].astype(F32)
                mine += crossed[2 * rest : 2 * rest + 2 * tall, cols].astype(F32)
                final[2 * rest : 2 * rest + 2 * tall, cols] = mine.astype(BF)

            each(piece * 3, piece * 3 + 3, columns)
        if number == EXTRAS:
            count = chips * EXTRA
            row, col = iota((chips * 8, count), 1), iota((chips * 8, count), 0)
            origin = lax.div(row, 2) * 8 + lax.rem(row, 2)
            total = jnp.zeros((chips * 8, quarter), F32)
            for q in range(QUARTERS):
                cols = slice(q * quarter, (q + 1) * quarter)
                spare = jnp.concatenate(
                    [final[2 * rest + (o + 1) * tall - MAIN : 2 * rest + (o + 1) * tall, cols] for o in range(2)], axis=0)
                total += nn((col == origin + EXTRA * q).astype(F32).astype(BF), spare)
            home_extra_out[...] = total.astype(BF).reshape(chips, 8, quarter)
            for k in range(chips):
                if k != OWN:
                    extra_home(k).start()
            home_extra[chip] = home_extra_out[OWN]
        for k in chunk_slots(number):
            if k != OWN:
                go_home(k).start()
            else:
                owner, place_in = divmod(k - first_k, n // 2)
                row = 2 * rest + owner * tall + place_in * MAIN
                home[slot_rows(chip), :] = final[row : row + MAIN, :]

    part = heads * DH // 2
    pieces = part // chips
    half_mine = pl.ds(pl.multiple_of(core * part, MAIN), part)
    half_other = pl.ds(pl.multiple_of((1 - core) * part, MAIN), part)

    class Scan:
        def __init__(self, reverse, own, result, swap, summed, got, made, prefix, onward, send, recv):
            self.reverse, self.own, self.result = reverse, own, result
            self.swap, self.summed, self.got, self.made = swap, summed, got, made
            self.prefix, self.onward, self.send, self.recv = prefix, onward, send, recv
            self.leads = core == (1 if reverse else 0)

        def trade(self):
            return pltpu.make_async_remote_copy(
                src_ref=self.own.at[half_other, :], dst_ref=self.swap, send_sem=self.send.at[0], recv_sem=self.recv.at[0],
                device_id={"ctx": partner}, device_id_type=MESH)

        def piece(self, number):
            return pl.ds(pl.multiple_of(number * pieces, MAIN), pieces)

        def out(self, stage, k):
            peer = lax.rem(chip + k, chips)
            source, target = ((self.summed, self.got), (self.made, self.prefix))[stage]
            return pltpu.make_async_remote_copy(
                src_ref=source.at[self.piece(peer), :], dst_ref=target.at[self.piece(chip), :],
                send_sem=self.send.at[1 + stage], recv_sem=self.recv.at[1 + stage],
                device_id={"ctx": peer * 2 + core}, device_id_type=MESH)

        def whole(self, stage):
            source, target = ((self.summed, self.got), (self.made, self.prefix))[stage]
            rows = pl.ds(0, (chips - 1) * pieces)
            return pltpu.make_async_remote_copy(
                src_ref=source.at[rows, :], dst_ref=target.at[rows, :],
                send_sem=self.send.at[1 + stage], recv_sem=self.recv.at[1 + stage],
                device_id={"ctx": partner}, device_id_type=MESH)

        def hand(self):
            return pltpu.make_async_remote_copy(
                src_ref=self.onward, dst_ref=self.result.at[half_mine, :], send_sem=self.send.at[3], recv_sem=self.recv.at[3],
                device_id={"ctx": partner}, device_id_type=MESH)

        def lead_rows(self, j):
            rows = pl.ds(j * DH, DH)
            own = self.own[pl.ds(pl.multiple_of(core * part + j * DH, DH), DH), :].astype(F32)
            other = self.swap[rows, :].astype(F32)
            fade = jnp.exp(jnp.full((DH, DH), -rates[core * (heads // 2) + j] * float(block), F32))
            first_one = jnp.where(self.leads, own, other)
            return rows, own, other, fade, first_one

        def join(self):
            self.trade().wait_recv()
            for j in range(heads // 2):
                rows, own, other, fade, first_one = self.lead_rows(j)
                self.summed[rows, :] = (fade * first_one + jnp.where(self.leads, other, own)).astype(BF)
            each(1, chips, lambda k: self.out(0, k).start())
            self.got[self.piece(chip), :] = self.summed[self.piece(chip), :]

        def run(self):
            row = iota((pieces, DH), 0) + chip * pieces
            rate = jnp.zeros((pieces, DH), F32)
            for j in range(heads // 2):
                rate = jnp.where((row >= j * DH) & (row < (j + 1) * DH), rates[core * (heads // 2) + j], rate)
            factor = jnp.exp(-rate * float(2 * block))
            self.whole(0).wait_recv()
            total = jnp.zeros((pieces, DH), F32)
            for i in range(chips):
                c = chips - 1 - i if self.reverse else i
                self.made[c * pieces : (c + 1) * pieces, :] = total.astype(BF)
                total = factor * total + self.got[c * pieces : (c + 1) * pieces, :].astype(F32)
            each(1, chips, lambda k: self.out(1, k).start())
            self.prefix[self.piece(chip), :] = self.made[self.piece(chip), :]

        def split(self):
            self.whole(1).wait_recv()
            for j in range(heads // 2):
                rows, _, _, fade, first_one = self.lead_rows(j)
                here = self.prefix[rows, :].astype(F32)
                after = fade * here + first_one
                self.onward[rows, :] = jnp.where(self.leads, after, here).astype(BF)
                target = pl.ds(pl.multiple_of(core * part + j * DH, DH), DH)
                self.result[target, :] = jnp.where(self.leads, here, after).astype(BF)
            self.hand().start()

        def done(self):
            self.hand().wait_recv()

        def sent(self):
            self.trade().wait_send()
            self.whole(0).wait_send()
            self.whole(1).wait_send()
            self.hand().wait_send()

    fore = Scan(False, local, entering, swap, summed, got, made, prefix, onward, fore_s, fore_r)
    rear = Scan(True, local_b, leaving, swap_b, summed_b, got_b, made_b, prefix_b, onward_b, rear_s, rear_r)
    place = iota((block, DH), 0).astype(F32)

    def write_out(i):
        source, target = ((query_g, query_out), (key_g, key_out), (value_g, value_out))[i]
        return pltpu.make_async_copy(source, target, out_sem.at[i])

    def head_cols(h):
        return slice(h * DH, (h + 1) * DH)

    def scan_trade(path):
        path.trade().start()

    def scan_join(path):
        path.join()

    def scan_run(path):
        path.run()

    def scan_split(path):
        path.split()

    def scan_done(path):
        path.done()

    def within(h):
        distance = (iota((block, block), 0) - iota((block, block), 1)).astype(F32)
        return jnp.where(distance >= 0.0, jnp.exp(-rates[h] * jnp.maximum(distance, 0.0)), 0.0)

    loads[1].wait()
    gather(0, out_grad)
    for i in (2, 3, 4):
        loads[i].wait()
    for h in range(heads):
        faded = (keys[:, head_cols(h)].astype(F32) * jnp.exp(-rates[h] * (float(block) - place))).astype(BF)
        local[h * DH : (h + 1) * DH, :] = tn(faded, values[:, head_cols(h)]).astype(BF)
    pl.semaphore_wait(barrier, ctx - 1 + 2)
    scan_trade(fore)
    send_rows(0, MID)
    for i in (5, 6):
        loads[i].wait()
    for k in range(2):
        gates[:, k : k + 1] = upright(gate_rows[k : k + 1, :])

    def inside(h):
        score = nt(queries[:, head_cols(h)], keys[:, head_cols(h)])
        weight = (scale * score * within(h)).astype(BF)
        weights[h] = weight
        intra[:, head_cols(h)] = nn(weight, values[:, head_cols(h)])

    for h in range(heads // 2):
        inside(h)
    scan_join(fore)
    for h in range(heads // 2, heads):
        inside(h)
    send_rows(0, NEAR)
    pass_on(0, MID)
    scan_run(fore)
    send_rows(0, FAR)
    all_rows(0, MID)
    loads[7].wait()
    expert_in(0, MID)
    pass_on(0, NEAR)
    scan_split(fore)
    all_rows(0, NEAR)
    scan_done(fore)
    for h in range(heads):
        across = nn(queries[:, head_cols(h)], entering[h * DH : (h + 1) * DH, :])
        total = intra[:, head_cols(h)] + scale * jnp.exp(-rates[h] * place) * across
        attn[:, head_cols(h)] = total.astype(BF)
    gather(1, attn)
    send_rows(1, FAR)
    send_rows(1, MID)
    send_rows(1, NEAR)
    reduce_turn(0, MID)
    expert_in(0, NEAR)
    pass_on(0, FAR)
    all_rows(0, FAR)
    expert_in(0, FAR)
    reduce_turn(0, NEAR)
    pass_on(1, FAR)
    all_rows(1, FAR)
    loads[8].wait()
    expert_in(1, FAR)
    reduce_turn(0, FAR)
    pass_on(1, MID)
    all_rows(1, MID)
    expert_in(1, MID)
    pass_on(1, NEAR)
    reduce_turn(1, FAR)
    all_rows(1, NEAR)
    expert_in(1, NEAR)
    reduce_turn(1, MID)
    finish(FAR)
    reduce_turn(1, NEAR)
    spread_on(FAR)
    finish(MID)
    spread_done(FAR)
    spread_on(MID)
    finish(NEAR)
    expert_back(FAR)
    return_rows(FAR)
    spread_done(MID)
    expert_back(MID, (0,))
    spread_on(NEAR)
    expert_back(MID, (1,))
    return_rows(MID)
    for a in range(2):
        dispatch_extra_all(a).wait_send()
        relay_extra(a).wait_send()
        sent = send_main.at[a, pl.ds(0, (chips - 1) * MAIN), :]
        pltpu.make_async_remote_copy(
            src_ref=sent, dst_ref=sent, send_sem=main_s.at[a], recv_sem=main_r.at[a, 0],
            device_id={"ctx": partner}, device_id_type=MESH).wait_send()
        for number in range(len(CHUNKS)):
            relay_all(a, number).wait_send()
            for which in ("turn_up", "turn_down", "own_up", "own_down", "sum_up", "sum_down"):
                reducer(a, number, which).wait_send()
    fore.sent()
    spread_done(NEAR)
    expert_back(NEAR)
    return_rows(NEAR)

    extra_home_all().wait_recv()
    home_all().wait_recv()
    for q in range(QUARTERS):
        cols = slice(q * quarter, (q + 1) * quarter)
        total = out_grad[:, cols].astype(F32)
        for k in range(2):
            mine = nn(main_hot[k], home[:, cols])
            mine += nn(extra_hot[k, q], home_extra[...].reshape(chips * 8, quarter))
            total += gates[:, k : k + 1] * mine
        grad_out[:, cols] = total.astype(BF)
    for h in range(heads):
        faded = (queries[:, head_cols(h)].astype(F32) * jnp.exp(-rates[h] * (place + 1.0))).astype(BF)
        local_b[h * DH : (h + 1) * DH, :] = tn(faded, grad_out[:, head_cols(h)]).astype(BF)
    scan_trade(rear)
    for h in range(heads):
        if h == heads // 3:
            scan_join(rear)
        cols = head_cols(h)
        grad = grad_out[:, cols]
        dweight = (scale * nt(grad, values[:, cols]) * within(h)).astype(BF)
        across = nt(grad, entering[h * DH : (h + 1) * DH, :])
        query_g[:, cols] = (nn(dweight, keys[:, cols]) + scale * jnp.exp(-rates[h] * place) * across).astype(BF)
        key_part[:, cols] = tn(dweight, queries[:, cols])
        value_part[:, cols] = tn(weights[h], grad)
    write_out(0).start()
    scan_run(rear)
    extra_home_all().wait_send()
    home_all().wait_send()
    for number in range(len(CHUNKS)):
        for piece in range(2):
            cross(number, 1 - core, piece).wait_send()
        for which in ("up_low", "up_high", "down_high", "down_low", "on_up", "on_down"):
            spread(number, which).wait_send()
    for h in range(heads):
        cols = head_cols(h)
        fade = scale * jnp.exp(-rates[h] * (float(block) - 1.0 - place))
        attn[:, cols] = (fade * values[:, cols].astype(F32)).astype(BF)
        faded_keys[:, cols] = (fade * keys[:, cols].astype(F32)).astype(BF)
    scan_split(rear)
    scan_done(rear)
    for h in range(heads):
        cols = head_cols(h)
        state = leaving[h * DH : (h + 1) * DH, :]
        key_g[:, cols] = (key_part[:, cols] + nt(attn[:, cols], state)).astype(BF)
    write_out(1).start()
    for h in range(heads):
        cols = head_cols(h)
        state = leaving[h * DH : (h + 1) * DH, :]
        value_g[:, cols] = (value_part[:, cols] + nn(faded_keys[:, cols], state)).astype(BF)
    write_out(2).start()
    for i in range(3):
        write_out(i).wait()

    rear.sent()


def leave_kernel(first, second, third, first_out, second_out, third_out, held, sems):
    sources, targets = (first, second, third), (first_out, second_out, third_out)
    inward = [pltpu.make_async_copy(sources[i], held.at[i], sems.at[0, i]) for i in range(3)]
    outward = [pltpu.make_async_copy(held.at[i], targets[i], sems.at[1, i]) for i in range(3)]
    for copy in inward:
        copy.start()
    for before, after in zip(inward, outward):
        before.wait()
        after.start()
    for copy in outward:
        copy.wait()


def on_device(
    queries, keys, values, out_grad, up_weight, down_weight, decay_rates, routes, gate_weights
):
    block, group = queries.shape
    heads = group // DH
    hidden = up_weight.shape[2]
    ctx = lax.axis_size("ctx")
    chips = ctx // 2
    slots = chips * MAIN
    total = 2 * chips * (MAIN + EXTRA)
    quarter = group // QUARTERS
    count = len(CHUNKS)
    state = (heads * DH, DH)
    dma = pltpu.SemaphoreType.DMA
    raw = pl.BlockSpec(memory_space=pl.ANY)
    out = jax.ShapeDtypeStruct((block, group), BF)
    grads = pl.pallas_call(
        layer_kernel,
        out_shape=(out, out, out),
        in_specs=[raw] * 9,
        out_specs=(raw, raw, raw),
        scratch_shapes=[pltpu.VMEM((block, group), BF)] * 3
        + [
            pltpu.SMEM((heads,), F32),
            pltpu.VMEM((2, block), jnp.int32),
            pltpu.VMEM((2, block), F32),
        ]
        + [pltpu.VMEM((block, group), BF)] * 4
        + [
            pltpu.VMEM((block, 2), F32),
            pltpu.VMEM((group, hidden), BF),
            pltpu.VMEM((hidden, group), BF),
            pltpu.VMEM((2, block, slots), BF),
            pltpu.VMEM((2, QUARTERS, block, chips * 8), BF),
            pltpu.VMEM((2, slots, group), BF),
            pltpu.VMEM((2, chips, 8, quarter), BF),
            pltpu.VMEM((2, total, group), BF),
            pltpu.VMEM((2, 2 * chips, 8, quarter), BF),
            pltpu.VMEM((2, total, hidden), BF),
            pltpu.VMEM((2, total // 4, hidden), BF),
            pltpu.VMEM((2, total // 4, hidden), BF),
            pltpu.VMEM((2, total // 4, hidden), BF),
            pltpu.VMEM((total, hidden), BF),
            pltpu.VMEM((total, group), BF),
            pltpu.VMEM((total // 2, group), BF),
            pltpu.VMEM((total // 2, group), BF),
            pltpu.VMEM((chips, 8, quarter), BF),
            pltpu.VMEM((slots, group), BF),
            pltpu.VMEM((chips, 8, quarter), BF),
            pltpu.VMEM((heads, block, block), BF),
            pltpu.VMEM((block, group), F32),
            pltpu.VMEM((block, group), BF),
        ]
        + [pltpu.VMEM(state, BF)] * 4
        + [pltpu.VMEM((heads * DH // 2, DH), BF)] * 12
        + [
            pltpu.VMEM((block, group), BF),
            pltpu.VMEM((block, group), F32),
            pltpu.VMEM((block, group), F32),
            pltpu.VMEM((block, group), BF),
            dma((9,)), dma((3,)),
            dma((2,)), dma((2, chips)),
            dma((2, count)), dma((2, count)),
        ]
        + [dma((2,))] * 4
        + [dma((4,))] * 4
        + [dma((2, count, 6))] * 2
        + [dma((count, 6))] * 2
        + [dma((count, 2))] * 2
        + [dma((1,))] * 4,
        compiler_params=pltpu.CompilerParams(
            collective_id=0, has_side_effects=True, vmem_limit_bytes=67043328
        ),
    )(decay_rates, routes.T, gate_weights.T, queries, keys, values, out_grad, up_weight, down_weight)
    return pl.pallas_call(
        leave_kernel,
        out_shape=(out, out, out),
        in_specs=[raw] * 3,
        out_specs=(raw, raw, raw),
        scratch_shapes=[pltpu.VMEM((3, block, group), BF), dma((2, 3))],
    )(*grads)


def solution(mesh):
    placed = (
        P("ctx", "exp"),
        P("ctx", "exp"),
        P("ctx", "exp"),
        P("ctx", "exp"),
        P("ctx", "exp", None),
        P("ctx", None, "exp"),
        P("exp"),
        P("ctx", None),
        P("ctx", None),
    )
    return jax.shard_map(
        on_device,
        mesh=mesh,
        in_specs=placed,
        out_specs=(P("ctx", "exp"), P("ctx", "exp"), P("ctx", "exp")),
        check_vma=False,
    )
```

```python
import jax
import jax.numpy as jnp
from jax import lax
from jax.experimental import pallas as pl
from jax.experimental.pallas import tpu as pltpu
from jax.sharding import PartitionSpec as P

DH = 128
MESH = pl.DeviceIdType.MESH
BF = jnp.bfloat16
F32 = jnp.float32
MID, FAR, NEAR = 0, 1, 2
CHUNKS = (6, 6, 4)
OFFSETS = (
    (3, 0), (1, 1), (1, 3), (3, 1), (3, 3), (0, 2),
    (2, 0), (1, 2), (3, 2), (2, 1), (2, 3), (2, 2),
    (0, 0), (0, 1), (0, 3), (1, 0),
)
OWN = OFFSETS.index((0, 0))
EXTRAS = FAR
MAIN = 16
EXTRA = 2
QUARTERS = 4


def nn(left, right):
    return lax.dot_general(left, right, (((1,), (0,)), ((), ())), preferred_element_type=F32)


def nt(left, right):
    return lax.dot_general(left, right, (((1,), (1,)), ((), ())), preferred_element_type=F32)


def tn(left, right):
    return lax.dot_general(left, right, (((0,), (0,)), ((), ())), preferred_element_type=F32)


def iota(shape, dim):
    return lax.broadcasted_iota(jnp.int32, shape, dim)


def each(lower, upper, action):
    def body(i, carry):
        action(i)
        return carry

    lax.fori_loop(lower, upper, body, 0)


def layer_kernel(
    rates_hbm, routes_hbm, gates_hbm, queries_hbm, keys_hbm, values_hbm, out_grad_hbm, up_hbm, down_hbm,
    query_out, key_out, value_out,
    query_g, key_g, value_g, rates, route_rows, gate_rows, queries, keys, values, out_grad, gates,
    up, down, main_hot, extra_hot, main_pick, extra_pick, send_main, send_extra, rows_in, extra_in, partial,
    turned, below, above, slope, back, crossed, final, home_extra_out, home, home_extra,
    weights, intra, attn, local, entering, local_b, leaving, swap, summed, got, made, prefix, onward,
    swap_b, summed_b, got_b, made_b, prefix_b, onward_b, grad_out,
    key_part, value_part, faded_keys,
    load_sem, out_sem, main_s, main_r, relay_s, relay_r, extra_s, extra_r, hop_s, hop_r,
    fore_s, fore_r, rear_s, rear_r, reduce_s, reduce_r, gather_s, gather_r, cross_s, cross_r,
    home_s, home_r, homex_s, homex_r,
):
    block = queries.shape[0]
    group = queries.shape[1]
    heads = group // DH
    hidden = up.shape[1]
    half = hidden // 2
    quarter = group // QUARTERS
    scale = 1.0 / DH
    ctx = lax.axis_size("ctx")
    chips = ctx // 2
    me = lax.axis_index("ctx")
    level = lax.axis_index("exp")
    chip = lax.div(me, 2)
    core = lax.rem(me, 2)
    partner = me + 1 - 2 * core
    nxt, opp, prv = (lax.rem(level + i, 4) for i in (1, 2, 3))

    barrier = pltpu.get_barrier_semaphore()
    each(1, ctx, lambda k: pl.semaphore_signal(
        barrier, inc=1, device_id={"ctx": lax.rem(me + k, ctx)}, device_id_type=MESH))
    for peer in (nxt, prv):
        pl.semaphore_signal(barrier, inc=1, device_id={"exp": peer}, device_id_type=MESH)
    loads = [
        pltpu.make_async_copy(source, target, load_sem.at[i])
        for i, (source, target) in enumerate((
            (routes_hbm, route_rows), (out_grad_hbm, out_grad), (rates_hbm, rates), (keys_hbm, keys),
            (values_hbm, values), (queries_hbm, queries), (gates_hbm, gate_rows),
            (down_hbm.at[0], down), (up_hbm.at[0], up)))
    ]
    for load in loads:
        load.start()

    spans, base, short, first = [], 0, 0, 0
    for number, n in enumerate(CHUNKS):
        tall = 8 * n + (MAIN if number == EXTRAS else 0)
        spans.append((first, n, base, tall, short))
        first, base, short = first + n, base + 4 * tall, short + tall

    def block_row(k, side):
        number = sum(k >= first_k for first_k, *_ in spans) - 1
        first_k, n, start, tall, _ = spans[number]
        owner, place_in = divmod(k - first_k, n // 2)
        return pl.ds(pl.multiple_of(start + (2 * side + owner) * tall + place_in * MAIN, MAIN), MAIN)

    def chunk_slots(number):
        return range(spans[number][0], spans[number][0] + spans[number][1])

    loads[0].wait()
    diagonal = iota((block, block), 0) == iota((block, block), 1)

    def upright(row):
        return jnp.sum(jnp.where(diagonal, row, 0.0), axis=1, keepdims=True)

    routes = [upright(route_rows[k : k + 1, :].astype(F32)).astype(jnp.int32) for k in range(2)]
    expert = iota((block, chips), 1)
    hits = [(routes[k] == expert).astype(F32) for k in range(2)]
    earlier = (iota((block, block), 1) < iota((block, block), 0)).astype(BF)
    before = nn(earlier, (hits[0] + hits[1]).astype(BF))
    for k in range(2):
        placed = jnp.sum(before * hits[k], axis=1, keepdims=True).astype(jnp.int32)
        chosen = routes[k]
        target = jnp.where(placed < MAIN, chosen * MAIN + placed, -1)
        main_hot[k] = (target == iota((block, chips * MAIN), 1)).astype(F32).astype(BF)
        spare = jnp.where(placed >= MAIN, chosen * 8 + placed - MAIN, -64)
        for q in range(QUARTERS):
            extra_hot[k, q] = (spare + EXTRA * q == iota((block, chips * 8), 1)).astype(F32).astype(BF)

    unit = diagonal.astype(F32).astype(BF)
    main_pick[...] = tn(main_hot[0] + main_hot[1], unit).astype(BF)
    for q in range(QUARTERS):
        extra_pick[q] = tn(extra_hot[0, q] + extra_hot[1, q], unit).astype(BF)

    def gather(a, source):
        def columns(i):
            cols = pl.ds(pl.multiple_of(i * 256, 256), 256)
            send_main[a, :, cols] = nn(main_pick[...], source[:, cols]).astype(BF)

        each(0, group // 256, columns)
        total = jnp.zeros((chips * 8, quarter), F32)
        for q in range(QUARTERS):
            total += nn(extra_pick[q], source[:, q * quarter : (q + 1) * quarter])
        send_extra[a] = total.astype(BF).reshape(chips, 8, quarter)

    side_len = 4
    z, x = lax.div(chip, side_len), lax.rem(chip, side_len)

    def to_chip(k):
        dz, dx = OFFSETS[k]
        return lax.rem(z + dz, side_len) * side_len + lax.rem(x + dx, side_len)

    def from_chip(k):
        dz, dx = OFFSETS[k]
        return (lax.rem(z + side_len - dz, side_len) * side_len + lax.rem(x + side_len - dx, side_len)) * 2 + core

    def slot_rows(number):
        return pl.ds(pl.multiple_of(number * MAIN, MAIN), MAIN)

    def dispatch(a, k):
        return pltpu.make_async_remote_copy(
            src_ref=send_main.at[a, slot_rows(to_chip(k)), :], dst_ref=rows_in.at[a, block_row(k, core), :],
            send_sem=main_s.at[a], recv_sem=main_r.at[a, k],
            device_id={"ctx": to_chip(k) * 2 + core}, device_id_type=MESH)

    def relay(a, k, number):
        rows = rows_in.at[a, block_row(k, core), :]
        return pltpu.make_async_remote_copy(
            src_ref=rows, dst_ref=rows, send_sem=relay_s.at[a, number], recv_sem=relay_r.at[a, number],
            device_id={"ctx": partner}, device_id_type=MESH)

    def relay_all(a, number):
        rows = rows_in.at[a, pl.ds(spans[number][2], spans[number][1] * MAIN), :]
        return pltpu.make_async_remote_copy(
            src_ref=rows, dst_ref=rows, send_sem=relay_s.at[a, number], recv_sem=relay_r.at[a, number],
            device_id={"ctx": partner}, device_id_type=MESH)

    def dispatch_extra(a, k):
        return pltpu.make_async_remote_copy(
            src_ref=send_extra.at[a, to_chip(k)], dst_ref=extra_in.at[a, core * chips + k],
            send_sem=extra_s.at[a], recv_sem=extra_r.at[a],
            device_id={"ctx": to_chip(k) * 2 + core}, device_id_type=MESH)

    def dispatch_extra_all(a):
        return pltpu.make_async_remote_copy(
            src_ref=send_extra.at[a, pl.ds(0, chips - 1)], dst_ref=extra_in.at[a, pl.ds(0, chips - 1)],
            send_sem=extra_s.at[a], recv_sem=extra_r.at[a],
            device_id={"ctx": partner}, device_id_type=MESH)

    def relay_extra(a):
        rows = extra_in.at[a, pl.ds(core * chips, chips)]
        return pltpu.make_async_remote_copy(
            src_ref=rows, dst_ref=rows, send_sem=hop_s.at[a], recv_sem=hop_r.at[a],
            device_id={"ctx": partner}, device_id_type=MESH)

    def send_rows(a, number):
        if number == EXTRAS:
            for k in range(chips):
                if k != OWN:
                    dispatch_extra(a, k).start()
            extra_in[a, core * chips + OWN] = send_extra[a, chip]
        for k in chunk_slots(number):
            if k == OWN:
                rows_in[a, block_row(OWN, core), :] = send_main[a, slot_rows(chip), :]
                relay(a, OWN, number).start()
            else:
                dispatch(a, k).start()

    def pass_on(a, number):
        if number == EXTRAS:
            dispatch_extra_all(a).wait_recv()
            relay_extra(a).start()
        for k in chunk_slots(number):
            if k != OWN:
                dispatch(a, k).wait_recv()
                relay(a, k, number).start()

    def all_rows(a, number):
        _, _, start, tall, _ = spans[number]
        if number == EXTRAS:
            relay_extra(a).wait_recv()
            packed = extra_in[a].reshape(2 * chips * 8, quarter)
            count = 2 * chips * EXTRA
            row, col = iota((count, 2 * chips * 8), 0), iota((count, 2 * chips * 8), 1)
            origin = lax.div(row, 2) * 8 + lax.rem(row, 2)
            for q in range(QUARTERS):
                placed = nn((col == origin + EXTRA * q).astype(F32).astype(BF), packed).astype(BF)
                for owner in range(4):
                    at = start + owner * tall + tall - MAIN
                    rows_in[a, at : at + MAIN, q * quarter : (q + 1) * quarter] = placed[owner * MAIN : (owner + 1) * MAIN]
        relay_all(a, number).wait_recv()

    def expert_in(a, number):
        start, tall = spans[number][2:4]
        span = slice(start, start + 4 * tall)

        def block_of(at, wide):
            rows = rows_in[a, span, :]
            if a == 0:
                product = nt(rows, down[pl.ds(at, wide), :])
            else:
                product = nn(rows, up[:, pl.ds(at, wide)])
            partial[a, span, pl.ds(at, wide)] = product.astype(BF)

        for side, moves in enumerate((("turn_up", "own_down"), ("turn_down", "own_up"))):
            each(0, half // 256, lambda i: block_of(pl.multiple_of(side * half + i * 256, 128), 256))
            done = half // 256 * 256
            if done < half:
                block_of(side * half + done, half - done)
            for which in moves:
                reducer(a, number, which).start()

    low, high = pl.ds(0, half), pl.ds(half, half)

    def reducer(a, number, which):
        _, _, start, tall, rest = spans[number]

        def owned(by):
            return pl.ds(pl.multiple_of(start + by * tall, MAIN), tall)

        there = pl.ds(rest, tall)
        src, dst, peer = {
            "turn_up": ((owned(opp), low), (turned, 0, low), nxt),
            "turn_down": ((owned(opp), high), (turned, 0, high), prv),
            "own_up": ((owned(nxt), high), (below, 0, high), nxt),
            "own_down": ((owned(prv), low), (above, 0, low), prv),
            "sum_up": ((owned(nxt), low), (below, 0, low), nxt),
            "sum_down": ((owned(prv), high), (above, 0, high), prv),
        }[which]
        slot = ("turn_up", "turn_down", "own_up", "own_down", "sum_up", "sum_down").index(which)
        return pltpu.make_async_remote_copy(
            src_ref=partial.at[a, src[0], src[1]], dst_ref=dst[0].at[a, there, dst[2]],
            send_sem=reduce_s.at[a, number, slot], recv_sem=reduce_r.at[a, number, slot],
            device_id={"exp": peer}, device_id_type=MESH)

    def reduce_turn(a, number):
        _, _, start, tall, rest = spans[number]
        wide = half // 3
        for turn, onward, by, offset in (("turn_up", "sum_up", nxt, 0), ("turn_down", "sum_down", prv, half)):
            reducer(a, number, turn).wait_recv()
            rows = pl.ds(pl.multiple_of(start + by * tall, MAIN), tall)

            def columns(i):
                cols = pl.ds(pl.multiple_of(offset + i * wide, 128), wide)
                mine = partial[a, rows, cols].astype(F32) + turned[a, rest : rest + tall, cols].astype(F32)
                partial[a, rows, cols] = mine.astype(BF)

            each(0, 3, columns)
            reducer(a, number, onward).start()

    def finish(number):
        _, _, start, tall, rest = spans[number]
        for a in range(2):
            for which in ("own_up", "own_down", "sum_up", "sum_down"):
                reducer(a, number, which).wait_recv()
        rows = pl.ds(pl.multiple_of(start + level * tall, MAIN), tall)
        there = pl.ds(rest, tall)

        def columns(i):
            cols = pl.ds(pl.multiple_of(i * 384, 128), 384)

            def total(a):
                return (partial[a, rows, cols].astype(F32) + below[a, there, cols].astype(F32)
                        + above[a, there, cols].astype(F32))

            pre = total(1)
            sigma = jax.nn.sigmoid(pre)
            slope[rows, cols] = (total(0) * (sigma * (1.0 + pre * (1.0 - sigma)))).astype(BF)

        each(0, hidden // 384, columns)
        for which in ("up_low", "down_high", "up_high", "down_low"):
            spread(number, which).start()

    def spread(number, which):
        _, _, start, tall, _ = spans[number]

        def owned(by):
            return pl.ds(pl.multiple_of(start + by * tall, MAIN), tall)

        owner, cols, peer = {
            "up_low": (level, low, nxt),
            "up_high": (level, high, nxt),
            "down_high": (level, high, prv),
            "down_low": (level, low, prv),
            "on_up": (prv, low, nxt),
            "on_down": (nxt, high, prv),
        }[which]
        slot = ("up_low", "up_high", "down_high", "down_low", "on_up", "on_down").index(which)
        rows = slope.at[owned(owner), cols]
        return pltpu.make_async_remote_copy(
            src_ref=rows, dst_ref=rows,
            send_sem=gather_s.at[number, slot], recv_sem=gather_r.at[number, slot],
            device_id={"exp": peer}, device_id_type=MESH)

    def spread_on(number):
        spread(number, "up_low").wait_recv()
        spread(number, "on_up").start()
        spread(number, "down_high").wait_recv()
        spread(number, "on_down").start()

    def spread_done(number):
        for which in ("up_high", "down_low", "on_up", "on_down"):
            spread(number, which).wait_recv()

    def cross(number, side, piece):
        _, _, start, tall, rest = spans[number]
        cols = pl.ds(piece * (group // 2), group // 2)
        return pltpu.make_async_remote_copy(
            src_ref=back.at[pl.ds(pl.multiple_of(start + side * 2 * tall, MAIN), 2 * tall), cols],
            dst_ref=crossed.at[pl.ds(2 * rest, 2 * tall), cols],
            send_sem=cross_s.at[number, piece], recv_sem=cross_r.at[number, piece],
            device_id={"ctx": partner}, device_id_type=MESH)

    def expert_back(number, pieces_of=(0, 1)):
        _, _, start, tall, _ = spans[number]

        def columns(i):
            at = pl.multiple_of(i * 256, 256)
            product = nt(slope[start : start + 4 * tall, :], up[pl.ds(at, 256), :])
            back[start : start + 4 * tall, pl.ds(at, 256)] = product.astype(BF)

        for piece in pieces_of:
            each(piece * 3, piece * 3 + 3, columns)
            cross(number, 1 - core, piece).start()

    def go_home(k):
        number = sum(k >= first_k for first_k, *_ in spans) - 1
        first_k, n, _, tall, rest = spans[number]
        owner, place_in = divmod(k - first_k, n // 2)
        row = 2 * rest + owner * tall + place_in * MAIN
        return pltpu.make_async_remote_copy(
            src_ref=final.at[pl.ds(row, MAIN), :], dst_ref=home.at[slot_rows(chip), :],
            send_sem=home_s.at[0], recv_sem=home_r.at[0],
            device_id={"ctx": from_chip(k)}, device_id_type=MESH)

    def home_all():
        rows = pl.ds(0, (chips - 1) * MAIN)
        return pltpu.make_async_remote_copy(
            src_ref=final.at[rows, :], dst_ref=home.at[rows, :], send_sem=home_s.at[0], recv_sem=home_r.at[0],
            device_id={"ctx": partner}, device_id_type=MESH)

    def extra_home(k):
        return pltpu.make_async_remote_copy(
            src_ref=home_extra_out.at[k], dst_ref=home_extra.at[chip],
            send_sem=homex_s.at[0], recv_sem=homex_r.at[0],
            device_id={"ctx": from_chip(k)}, device_id_type=MESH)

    def extra_home_all():
        rows = pl.ds(0, chips - 1)
        return pltpu.make_async_remote_copy(
            src_ref=home_extra_out.at[rows], dst_ref=home_extra.at[rows],
            send_sem=homex_s.at[0], recv_sem=homex_r.at[0],
            device_id={"ctx": partner}, device_id_type=MESH)

    def return_rows(number):
        first_k, n, start, tall, rest = spans[number]
        own = pl.multiple_of(start + core * 2 * tall, MAIN)
        for piece in range(2):
            cross(number, core, piece).wait_recv()

            def columns(i):
                cols = pl.ds(pl.multiple_of(i * 256, 256), 256)
                mine = back[pl.ds(own, 2 * tall), cols].astype(F32)
                mine += crossed[2 * rest : 2 * rest + 2 * tall, cols].astype(F32)
                final[2 * rest : 2 * rest + 2 * tall, cols] = mine.astype(BF)

            each(piece * 3, piece * 3 + 3, columns)
        if number == EXTRAS:
            count = chips * EXTRA
            row, col = iota((chips * 8, count), 1), iota((chips * 8, count), 0)
            origin = lax.div(row, 2) * 8 + lax.rem(row, 2)
            total = jnp.zeros((chips * 8, quarter), F32)
            for q in range(QUARTERS):
                cols = slice(q * quarter, (q + 1) * quarter)
                spare = jnp.concatenate(
                    [final[2 * rest + (o + 1) * tall - MAIN : 2 * rest + (o + 1) * tall, cols] for o in range(2)], axis=0)
                total += nn((col == origin + EXTRA * q).astype(F32).astype(BF), spare)
            home_extra_out[...] = total.astype(BF).reshape(chips, 8, quarter)
            for k in range(chips):
                if k != OWN:
                    extra_home(k).start()
            home_extra[chip] = home_extra_out[OWN]
        for k in chunk_slots(number):
            if k != OWN:
                go_home(k).start()
            else:
                owner, place_in = divmod(k - first_k, n // 2)
                row = 2 * rest + owner * tall + place_in * MAIN
                home[slot_rows(chip), :] = final[row : row + MAIN, :]

    part = heads * DH // 2
    pieces = part // chips
    half_mine = pl.ds(pl.multiple_of(core * part, MAIN), part)
    half_other = pl.ds(pl.multiple_of((1 - core) * part, MAIN), part)

    class Scan:
        def __init__(self, reverse, own, result, swap, summed, got, made, prefix, onward, send, recv):
            self.reverse, self.own, self.result = reverse, own, result
            self.swap, self.summed, self.got, self.made = swap, summed, got, made
            self.prefix, self.onward, self.send, self.recv = prefix, onward, send, recv
            self.leads = core == (1 if reverse else 0)

        def trade(self):
            return pltpu.make_async_remote_copy(
                src_ref=self.own.at[half_other, :], dst_ref=self.swap, send_sem=self.send.at[0], recv_sem=self.recv.at[0],
                device_id={"ctx": partner}, device_id_type=MESH)

        def piece(self, number):
            return pl.ds(pl.multiple_of(number * pieces, MAIN), pieces)

        def out(self, stage, k):
            peer = lax.rem(chip + k, chips)
            source, target = ((self.summed, self.got), (self.made, self.prefix))[stage]
            return pltpu.make_async_remote_copy(
                src_ref=source.at[self.piece(peer), :], dst_ref=target.at[self.piece(chip), :],
                send_sem=self.send.at[1 + stage], recv_sem=self.recv.at[1 + stage],
                device_id={"ctx": peer * 2 + core}, device_id_type=MESH)

        def whole(self, stage):
            source, target = ((self.summed, self.got), (self.made, self.prefix))[stage]
            rows = pl.ds(0, (chips - 1) * pieces)
            return pltpu.make_async_remote_copy(
                src_ref=source.at[rows, :], dst_ref=target.at[rows, :],
                send_sem=self.send.at[1 + stage], recv_sem=self.recv.at[1 + stage],
                device_id={"ctx": partner}, device_id_type=MESH)

        def hand(self):
            return pltpu.make_async_remote_copy(
                src_ref=self.onward, dst_ref=self.result.at[half_mine, :], send_sem=self.send.at[3], recv_sem=self.recv.at[3],
                device_id={"ctx": partner}, device_id_type=MESH)

        def lead_rows(self, j):
            rows = pl.ds(j * DH, DH)
            own = self.own[pl.ds(pl.multiple_of(core * part + j * DH, DH), DH), :].astype(F32)
            other = self.swap[rows, :].astype(F32)
            fade = jnp.exp(jnp.full((DH, DH), -rates[core * (heads // 2) + j] * float(block), F32))
            first_one = jnp.where(self.leads, own, other)
            return rows, own, other, fade, first_one

        def join(self):
            self.trade().wait_recv()
            for j in range(heads // 2):
                rows, own, other, fade, first_one = self.lead_rows(j)
                self.summed[rows, :] = (fade * first_one + jnp.where(self.leads, other, own)).astype(BF)
            each(1, chips, lambda k: self.out(0, k).start())
            self.got[self.piece(chip), :] = self.summed[self.piece(chip), :]

        def run(self):
            row = iota((pieces, DH), 0) + chip * pieces
            rate = jnp.zeros((pieces, DH), F32)
            for j in range(heads // 2):
                rate = jnp.where((row >= j * DH) & (row < (j + 1) * DH), rates[core * (heads // 2) + j], rate)
            factor = jnp.exp(-rate * float(2 * block))
            self.whole(0).wait_recv()
            total = jnp.zeros((pieces, DH), F32)
            for i in range(chips):
                c = chips - 1 - i if self.reverse else i
                self.made[c * pieces : (c + 1) * pieces, :] = total.astype(BF)
                total = factor * total + self.got[c * pieces : (c + 1) * pieces, :].astype(F32)
            each(1, chips, lambda k: self.out(1, k).start())
            self.prefix[self.piece(chip), :] = self.made[self.piece(chip), :]

        def split(self):
            self.whole(1).wait_recv()
            for j in range(heads // 2):
                rows, _, _, fade, first_one = self.lead_rows(j)
                here = self.prefix[rows, :].astype(F32)
                after = fade * here + first_one
                self.onward[rows, :] = jnp.where(self.leads, after, here).astype(BF)
                target = pl.ds(pl.multiple_of(core * part + j * DH, DH), DH)
                self.result[target, :] = jnp.where(self.leads, here, after).astype(BF)
            self.hand().start()

        def done(self):
            self.hand().wait_recv()

        def sent(self):
            self.trade().wait_send()
            self.whole(0).wait_send()
            self.whole(1).wait_send()
            self.hand().wait_send()

    fore = Scan(False, local, entering, swap, summed, got, made, prefix, onward, fore_s, fore_r)
    rear = Scan(True, local_b, leaving, swap_b, summed_b, got_b, made_b, prefix_b, onward_b, rear_s, rear_r)
    place = iota((block, DH), 0).astype(F32)

    def write_out(i):
        source, target = ((query_g, query_out), (key_g, key_out), (value_g, value_out))[i]
        return pltpu.make_async_copy(source, target, out_sem.at[i])

    def head_cols(h):
        return slice(h * DH, (h + 1) * DH)

    def scan_trade(path):
        path.trade().start()

    def scan_join(path):
        path.join()

    def scan_run(path):
        path.run()

    def scan_split(path):
        path.split()

    def scan_done(path):
        path.done()

    def within(h):
        distance = (iota((block, block), 0) - iota((block, block), 1)).astype(F32)
        return jnp.where(distance >= 0.0, jnp.exp(-rates[h] * jnp.maximum(distance, 0.0)), 0.0)

    loads[1].wait()
    gather(0, out_grad)
    for i in (2, 3, 4):
        loads[i].wait()
    for h in range(heads):
        faded = (keys[:, head_cols(h)].astype(F32) * jnp.exp(-rates[h] * (float(block) - place))).astype(BF)
        local[h * DH : (h + 1) * DH, :] = tn(faded, values[:, head_cols(h)]).astype(BF)
    pl.semaphore_wait(barrier, ctx - 1 + 2)
    scan_trade(fore)
    for i in (5, 6):
        loads[i].wait()
    for k in range(2):
        gates[:, k : k + 1] = upright(gate_rows[k : k + 1, :])

    def inside(h):
        score = nt(queries[:, head_cols(h)], keys[:, head_cols(h)])
        weight = (scale * score * within(h)).astype(BF)
        weights[h] = weight
        intra[:, head_cols(h)] = nn(weight, values[:, head_cols(h)])

    for h in range(heads // 2):
        inside(h)
    scan_join(fore)
    send_rows(0, MID)
    for h in range(heads // 2, heads):
        inside(h)
    scan_run(fore)
    send_rows(0, NEAR)
    pass_on(0, MID)
    send_rows(0, FAR)
    all_rows(0, MID)
    loads[7].wait()
    expert_in(0, MID)
    pass_on(0, NEAR)
    scan_split(fore)
    all_rows(0, NEAR)
    scan_done(fore)
    for h in range(heads):
        across = nn(queries[:, head_cols(h)], entering[h * DH : (h + 1) * DH, :])
        total = intra[:, head_cols(h)] + scale * jnp.exp(-rates[h] * place) * across
        attn[:, head_cols(h)] = total.astype(BF)
    gather(1, attn)
    send_rows(1, FAR)
    send_rows(1, MID)
    send_rows(1, NEAR)
    reduce_turn(0, MID)
    expert_in(0, NEAR)
    pass_on(0, FAR)
    all_rows(0, FAR)
    expert_in(0, FAR)
    reduce_turn(0, NEAR)
    pass_on(1, FAR)
    all_rows(1, FAR)
    loads[8].wait()
    expert_in(1, FAR)
    reduce_turn(0, FAR)
    pass_on(1, MID)
    all_rows(1, MID)
    expert_in(1, MID)
    pass_on(1, NEAR)
    reduce_turn(1, FAR)
    all_rows(1, NEAR)
    expert_in(1, NEAR)
    reduce_turn(1, MID)
    finish(FAR)
    reduce_turn(1, NEAR)
    spread_on(FAR)
    finish(MID)
    spread_done(FAR)
    spread_on(MID)
    finish(NEAR)
    expert_back(FAR)
    return_rows(FAR)
    spread_done(MID)
    expert_back(MID, (0,))
    spread_on(NEAR)
    expert_back(MID, (1,))
    return_rows(MID)
    for a in range(2):
        dispatch_extra_all(a).wait_send()
        relay_extra(a).wait_send()
        sent = send_main.at[a, pl.ds(0, (chips - 1) * MAIN), :]
        pltpu.make_async_remote_copy(
            src_ref=sent, dst_ref=sent, send_sem=main_s.at[a], recv_sem=main_r.at[a, 0],
            device_id={"ctx": partner}, device_id_type=MESH).wait_send()
        for number in range(len(CHUNKS)):
            relay_all(a, number).wait_send()
            for which in ("turn_up", "turn_down", "own_up", "own_down", "sum_up", "sum_down"):
                reducer(a, number, which).wait_send()
    fore.sent()
    spread_done(NEAR)
    expert_back(NEAR)
    return_rows(NEAR)

    extra_home_all().wait_recv()
    home_all().wait_recv()
    for q in range(QUARTERS):
        cols = slice(q * quarter, (q + 1) * quarter)
        total = out_grad[:, cols].astype(F32)
        for k in range(2):
            mine = nn(main_hot[k], home[:, cols])
            mine += nn(extra_hot[k, q], home_extra[...].reshape(chips * 8, quarter))
            total += gates[:, k : k + 1] * mine
        grad_out[:, cols] = total.astype(BF)
    for h in range(heads):
        faded = (queries[:, head_cols(h)].astype(F32) * jnp.exp(-rates[h] * (place + 1.0))).astype(BF)
        local_b[h * DH : (h + 1) * DH, :] = tn(faded, grad_out[:, head_cols(h)]).astype(BF)
    scan_trade(rear)
    for h in range(heads):
        if h == heads // 3:
            scan_join(rear)
        cols = head_cols(h)
        grad = grad_out[:, cols]
        dweight = (scale * nt(grad, values[:, cols]) * within(h)).astype(BF)
        across = nt(grad, entering[h * DH : (h + 1) * DH, :])
        query_g[:, cols] = (nn(dweight, keys[:, cols]) + scale * jnp.exp(-rates[h] * place) * across).astype(BF)
        key_part[:, cols] = tn(dweight, queries[:, cols])
        value_part[:, cols] = tn(weights[h], grad)
    write_out(0).start()
    scan_run(rear)
    extra_home_all().wait_send()
    home_all().wait_send()
    for number in range(len(CHUNKS)):
        for piece in range(2):
            cross(number, 1 - core, piece).wait_send()
        for which in ("up_low", "up_high", "down_high", "down_low", "on_up", "on_down"):
            spread(number, which).wait_send()
    for h in range(heads):
        cols = head_cols(h)
        fade = scale * jnp.exp(-rates[h] * (float(block) - 1.0 - place))
        attn[:, cols] = (fade * values[:, cols].astype(F32)).astype(BF)
        faded_keys[:, cols] = (fade * keys[:, cols].astype(F32)).astype(BF)
    scan_split(rear)
    scan_done(rear)
    for h in range(heads):
        cols = head_cols(h)
        state = leaving[h * DH : (h + 1) * DH, :]
        key_g[:, cols] = (key_part[:, cols] + nt(attn[:, cols], state)).astype(BF)
    write_out(1).start()
    for h in range(heads):
        cols = head_cols(h)
        state = leaving[h * DH : (h + 1) * DH, :]
        value_g[:, cols] = (value_part[:, cols] + nn(faded_keys[:, cols], state)).astype(BF)
    write_out(2).start()
    for i in range(3):
        write_out(i).wait()

    rear.sent()


def leave_kernel(first, second, third, first_out, second_out, third_out, sems):
    copies = [
        pltpu.make_async_copy(source, target, sems.at[i])
        for i, (source, target) in enumerate(((first, first_out), (second, second_out), (third, third_out)))
    ]
    for copy in copies:
        copy.start()
    for copy in copies:
        copy.wait()


def on_device(
    queries, keys, values, out_grad, up_weight, down_weight, decay_rates, routes, gate_weights
):
    block, group = queries.shape
    heads = group // DH
    hidden = up_weight.shape[2]
    ctx = lax.axis_size("ctx")
    chips = ctx // 2
    slots = chips * MAIN
    total = 2 * chips * (MAIN + EXTRA)
    quarter = group // QUARTERS
    count = len(CHUNKS)
    state = (heads * DH, DH)
    dma = pltpu.SemaphoreType.DMA
    raw = pl.BlockSpec(memory_space=pl.ANY)
    kept = pl.BlockSpec(memory_space=pltpu.HBM)
    out = jax.ShapeDtypeStruct((block, group), BF)
    grads = pl.pallas_call(
        layer_kernel,
        out_shape=(out, out, out),
        in_specs=[raw] * 9,
        out_specs=(raw, raw, raw),
        scratch_shapes=[pltpu.VMEM((block, group), BF)] * 3
        + [
            pltpu.SMEM((heads,), F32),
            pltpu.VMEM((2, block), jnp.int32),
            pltpu.VMEM((2, block), F32),
        ]
        + [pltpu.VMEM((block, group), BF)] * 4
        + [
            pltpu.VMEM((block, 2), F32),
            pltpu.VMEM((group, hidden), BF),
            pltpu.VMEM((hidden, group), BF),
            pltpu.VMEM((2, block, slots), BF),
            pltpu.VMEM((2, QUARTERS, block, chips * 8), BF),
            pltpu.VMEM((slots, block), BF),
            pltpu.VMEM((QUARTERS, chips * 8, block), BF),
            pltpu.VMEM((2, slots, group), BF),
            pltpu.VMEM((2, chips, 8, quarter), BF),
            pltpu.VMEM((2, total, group), BF),
            pltpu.VMEM((2, 2 * chips, 8, quarter), BF),
            pltpu.VMEM((2, total, hidden), BF),
            pltpu.VMEM((2, total // 4, hidden), BF),
            pltpu.VMEM((2, total // 4, hidden), BF),
            pltpu.VMEM((2, total // 4, hidden), BF),
            pltpu.VMEM((total, hidden), BF),
            pltpu.VMEM((total, group), BF),
            pltpu.VMEM((total // 2, group), BF),
            pltpu.VMEM((total // 2, group), BF),
            pltpu.VMEM((chips, 8, quarter), BF),
            pltpu.VMEM((slots, group), BF),
            pltpu.VMEM((chips, 8, quarter), BF),
            pltpu.VMEM((heads, block, block), BF),
            pltpu.VMEM((block, group), F32),
            pltpu.VMEM((block, group), BF),
        ]
        + [pltpu.VMEM(state, BF)] * 4
        + [pltpu.VMEM((heads * DH // 2, DH), BF)] * 12
        + [
            pltpu.VMEM((block, group), BF),
            pltpu.VMEM((block, group), F32),
            pltpu.VMEM((block, group), F32),
            pltpu.VMEM((block, group), BF),
            dma((9,)), dma((3,)),
            dma((2,)), dma((2, chips)),
            dma((2, count)), dma((2, count)),
        ]
        + [dma((2,))] * 4
        + [dma((4,))] * 4
        + [dma((2, count, 6))] * 2
        + [dma((count, 6))] * 2
        + [dma((count, 2))] * 2
        + [dma((1,))] * 4,
        compiler_params=pltpu.CompilerParams(
            collective_id=0, has_side_effects=True, vmem_limit_bytes=52 << 20
        ),
    )(decay_rates, routes.T, gate_weights.T, queries, keys, values, out_grad, up_weight, down_weight)
    return pl.pallas_call(
        leave_kernel,
        out_shape=(out, out, out),
        in_specs=[raw] * 3,
        out_specs=(kept, kept, kept),
        scratch_shapes=[dma((3,))],
        compiler_params=pltpu.CompilerParams(vmem_limit_bytes=1 << 20),
    )(*grads)


def solution(mesh):
    placed = (
        P("ctx", "exp"),
        P("ctx", "exp"),
        P("ctx", "exp"),
        P("ctx", "exp"),
        P("ctx", "exp", None),
        P("ctx", None, "exp"),
        P("exp"),
        P("ctx", None),
        P("ctx", None),
    )
    return jax.shard_map(
        on_device,
        mesh=mesh,
        in_specs=placed,
        out_specs=(P("ctx", "exp"), P("ctx", "exp"), P("ctx", "exp")),
        check_vma=False,
    )
```

```python
import jax
import jax.numpy as jnp
from jax import lax
from jax.experimental import pallas as pl
from jax.experimental.pallas import tpu as pltpu
from jax.sharding import PartitionSpec as P

DH = 128
MESH = pl.DeviceIdType.MESH
BF = jnp.bfloat16
F32 = jnp.float32
MID, FAR, NEAR = 0, 1, 2
CHUNKS = (6, 6, 4)
OFFSETS = (
    (3, 0), (1, 1), (1, 3), (3, 1), (3, 3), (0, 2),
    (2, 0), (1, 2), (3, 2), (2, 1), (2, 3), (2, 2),
    (0, 0), (0, 1), (0, 3), (1, 0),
)
OWN = OFFSETS.index((0, 0))
EXTRAS = FAR
MAIN = 16
EXTRA = 2
QUARTERS = 4


def nn(left, right):
    return lax.dot_general(left, right, (((1,), (0,)), ((), ())), preferred_element_type=F32)


def nt(left, right):
    return lax.dot_general(left, right, (((1,), (1,)), ((), ())), preferred_element_type=F32)


def tn(left, right):
    return lax.dot_general(left, right, (((0,), (0,)), ((), ())), preferred_element_type=F32)


def iota(shape, dim):
    return lax.broadcasted_iota(jnp.int32, shape, dim)


def each(lower, upper, action):
    def body(i, carry):
        action(i)
        return carry

    lax.fori_loop(lower, upper, body, 0)


def layer_kernel(
    rates_hbm, routes_hbm, gates_hbm, queries_hbm, keys_hbm, values_hbm, out_grad_hbm, up_hbm, down_hbm,
    query_out, key_out, value_out,
    query_g, key_g, value_g, rates, route_rows, gate_rows, queries, keys, values, out_grad, gates,
    up, down, main_hot, extra_hot, main_pick, extra_pick, send_main, send_extra, rows_in, extra_in, partial,
    turned, below, above, slope, back, crossed, final, home_extra_out, home, home_extra,
    weights, intra, attn, local, entering, local_b, leaving, swap, summed, got, made, prefix, onward,
    swap_b, summed_b, got_b, made_b, prefix_b, onward_b, grad_out,
    key_part, value_part, faded_keys,
    load_sem, out_sem, main_s, main_r, relay_s, relay_r, extra_s, extra_r, hop_s, hop_r,
    fore_s, fore_r, rear_s, rear_r, reduce_s, reduce_r, gather_s, gather_r, cross_s, cross_r,
    home_s, home_r, homex_s, homex_r,
):
    block = queries.shape[0]
    group = queries.shape[1]
    heads = group // DH
    hidden = up.shape[1]
    half = hidden // 2
    quarter = group // QUARTERS
    scale = 1.0 / DH
    ctx = lax.axis_size("ctx")
    chips = ctx // 2
    me = lax.axis_index("ctx")
    level = lax.axis_index("exp")
    chip = lax.div(me, 2)
    core = lax.rem(me, 2)
    partner = me + 1 - 2 * core
    nxt, opp, prv = (lax.rem(level + i, 4) for i in (1, 2, 3))

    barrier = pltpu.get_barrier_semaphore()
    each(1, ctx, lambda k: pl.semaphore_signal(
        barrier, inc=1, device_id={"ctx": lax.rem(me + k, ctx)}, device_id_type=MESH))
    for peer in (nxt, prv):
        pl.semaphore_signal(barrier, inc=1, device_id={"exp": peer}, device_id_type=MESH)
    loads = [
        pltpu.make_async_copy(source, target, load_sem.at[i])
        for i, (source, target) in enumerate((
            (routes_hbm, route_rows), (out_grad_hbm, out_grad), (rates_hbm, rates), (keys_hbm, keys),
            (values_hbm, values), (queries_hbm, queries), (gates_hbm, gate_rows),
            (down_hbm.at[0], down), (up_hbm.at[0], up)))
    ]
    for load in loads:
        load.start()

    spans, base, short, first = [], 0, 0, 0
    for number, n in enumerate(CHUNKS):
        tall = 8 * n + (MAIN if number == EXTRAS else 0)
        spans.append((first, n, base, tall, short))
        first, base, short = first + n, base + 4 * tall, short + tall

    def block_row(k, side):
        number = sum(k >= first_k for first_k, *_ in spans) - 1
        first_k, n, start, tall, _ = spans[number]
        owner, place_in = divmod(k - first_k, n // 2)
        return pl.ds(pl.multiple_of(start + (2 * side + owner) * tall + place_in * MAIN, MAIN), MAIN)

    def chunk_slots(number):
        return range(spans[number][0], spans[number][0] + spans[number][1])

    loads[0].wait()
    diagonal = iota((block, block), 0) == iota((block, block), 1)

    def upright(row):
        return jnp.sum(jnp.where(diagonal, row, 0.0), axis=1, keepdims=True)

    routes = [upright(route_rows[k : k + 1, :].astype(F32)).astype(jnp.int32) for k in range(2)]
    expert = iota((block, chips), 1)
    hits = [(routes[k] == expert).astype(F32) for k in range(2)]
    earlier = (iota((block, block), 1) < iota((block, block), 0)).astype(BF)
    before = nn(earlier, (hits[0] + hits[1]).astype(BF))
    for k in range(2):
        placed = jnp.sum(before * hits[k], axis=1, keepdims=True).astype(jnp.int32)
        chosen = routes[k]
        target = jnp.where(placed < MAIN, chosen * MAIN + placed, -1)
        main_hot[k] = (target == iota((block, chips * MAIN), 1)).astype(F32).astype(BF)
        spare = jnp.where(placed >= MAIN, chosen * 8 + placed - MAIN, -64)
        for q in range(QUARTERS):
            extra_hot[k, q] = (spare + EXTRA * q == iota((block, chips * 8), 1)).astype(F32).astype(BF)

    unit = diagonal.astype(F32).astype(BF)
    main_pick[...] = tn(main_hot[0] + main_hot[1], unit).astype(BF)
    for q in range(QUARTERS):
        extra_pick[q] = tn(extra_hot[0, q] + extra_hot[1, q], unit).astype(BF)

    def gather(a, source):
        def columns(i):
            cols = pl.ds(pl.multiple_of(i * 256, 256), 256)
            send_main[a, :, cols] = nn(main_pick[...], source[:, cols]).astype(BF)

        each(0, group // 256, columns)
        total = jnp.zeros((chips * 8, quarter), F32)
        for q in range(QUARTERS):
            total += nn(extra_pick[q], source[:, q * quarter : (q + 1) * quarter])
        send_extra[a] = total.astype(BF).reshape(chips, 8, quarter)

    side_len = 4
    z, x = lax.div(chip, side_len), lax.rem(chip, side_len)

    def to_chip(k):
        dz, dx = OFFSETS[k]
        return lax.rem(z + dz, side_len) * side_len + lax.rem(x + dx, side_len)

    def from_chip(k):
        dz, dx = OFFSETS[k]
        return (lax.rem(z + side_len - dz, side_len) * side_len + lax.rem(x + side_len - dx, side_len)) * 2 + core

    def slot_rows(number):
        return pl.ds(pl.multiple_of(number * MAIN, MAIN), MAIN)

    def dispatch(a, k):
        return pltpu.make_async_remote_copy(
            src_ref=send_main.at[a, slot_rows(to_chip(k)), :], dst_ref=rows_in.at[a, block_row(k, core), :],
            send_sem=main_s.at[a], recv_sem=main_r.at[a, k],
            device_id={"ctx": to_chip(k) * 2 + core}, device_id_type=MESH)

    def relay(a, k, number):
        rows = rows_in.at[a, block_row(k, core), :]
        return pltpu.make_async_remote_copy(
            src_ref=rows, dst_ref=rows, send_sem=relay_s.at[a, number], recv_sem=relay_r.at[a, number],
            device_id={"ctx": partner}, device_id_type=MESH)

    def relay_all(a, number):
        rows = rows_in.at[a, pl.ds(spans[number][2], spans[number][1] * MAIN), :]
        return pltpu.make_async_remote_copy(
            src_ref=rows, dst_ref=rows, send_sem=relay_s.at[a, number], recv_sem=relay_r.at[a, number],
            device_id={"ctx": partner}, device_id_type=MESH)

    def dispatch_extra(a, k):
        return pltpu.make_async_remote_copy(
            src_ref=send_extra.at[a, to_chip(k)], dst_ref=extra_in.at[a, core * chips + k],
            send_sem=extra_s.at[a], recv_sem=extra_r.at[a],
            device_id={"ctx": to_chip(k) * 2 + core}, device_id_type=MESH)

    def dispatch_extra_all(a):
        return pltpu.make_async_remote_copy(
            src_ref=send_extra.at[a, pl.ds(0, chips - 1)], dst_ref=extra_in.at[a, pl.ds(0, chips - 1)],
            send_sem=extra_s.at[a], recv_sem=extra_r.at[a],
            device_id={"ctx": partner}, device_id_type=MESH)

    def relay_extra(a):
        rows = extra_in.at[a, pl.ds(core * chips, chips)]
        return pltpu.make_async_remote_copy(
            src_ref=rows, dst_ref=rows, send_sem=hop_s.at[a], recv_sem=hop_r.at[a],
            device_id={"ctx": partner}, device_id_type=MESH)

    def send_rows(a, number):
        if number == EXTRAS:
            for k in range(chips):
                if k != OWN:
                    dispatch_extra(a, k).start()
            extra_in[a, core * chips + OWN] = send_extra[a, chip]
        for k in chunk_slots(number):
            if k == OWN:
                rows_in[a, block_row(OWN, core), :] = send_main[a, slot_rows(chip), :]
                relay(a, OWN, number).start()
            else:
                dispatch(a, k).start()

    def pass_on(a, number):
        if number == EXTRAS:
            dispatch_extra_all(a).wait_recv()
            relay_extra(a).start()
        for k in chunk_slots(number):
            if k != OWN:
                dispatch(a, k).wait_recv()
                relay(a, k, number).start()

    def all_rows(a, number):
        _, _, start, tall, _ = spans[number]
        if number == EXTRAS:
            relay_extra(a).wait_recv()
            packed = extra_in[a].reshape(2 * chips * 8, quarter)
            count = 2 * chips * EXTRA
            row, col = iota((count, 2 * chips * 8), 0), iota((count, 2 * chips * 8), 1)
            origin = lax.div(row, 2) * 8 + lax.rem(row, 2)
            for q in range(QUARTERS):
                placed = nn((col == origin + EXTRA * q).astype(F32).astype(BF), packed).astype(BF)
                for owner in range(4):
                    at = start + owner * tall + tall - MAIN
                    rows_in[a, at : at + MAIN, q * quarter : (q + 1) * quarter] = placed[owner * MAIN : (owner + 1) * MAIN]
        relay_all(a, number).wait_recv()

    def expert_in(a, number):
        start, tall = spans[number][2:4]
        span = slice(start, start + 4 * tall)

        def block_of(at, wide):
            rows = rows_in[a, span, :]
            if a == 0:
                product = nt(rows, down[pl.ds(at, wide), :])
            else:
                product = nn(rows, up[:, pl.ds(at, wide)])
            partial[a, span, pl.ds(at, wide)] = product.astype(BF)

        for side, moves in enumerate((("turn_up", "own_down"), ("turn_down", "own_up"))):
            each(0, half // 256, lambda i: block_of(pl.multiple_of(side * half + i * 256, 128), 256))
            done = half // 256 * 256
            if done < half:
                block_of(side * half + done, half - done)
            for which in moves:
                reducer(a, number, which).start()

    low, high = pl.ds(0, half), pl.ds(half, half)

    def reducer(a, number, which):
        _, _, start, tall, rest = spans[number]

        def owned(by):
            return pl.ds(pl.multiple_of(start + by * tall, MAIN), tall)

        there = pl.ds(rest, tall)
        src, dst, peer = {
            "turn_up": ((owned(opp), low), (turned, 0, low), nxt),
            "turn_down": ((owned(opp), high), (turned, 0, high), prv),
            "own_up": ((owned(nxt), high), (below, 0, high), nxt),
            "own_down": ((owned(prv), low), (above, 0, low), prv),
            "sum_up": ((owned(nxt), low), (below, 0, low), nxt),
            "sum_down": ((owned(prv), high), (above, 0, high), prv),
        }[which]
        slot = ("turn_up", "turn_down", "own_up", "own_down", "sum_up", "sum_down").index(which)
        return pltpu.make_async_remote_copy(
            src_ref=partial.at[a, src[0], src[1]], dst_ref=dst[0].at[a, there, dst[2]],
            send_sem=reduce_s.at[a, number, slot], recv_sem=reduce_r.at[a, number, slot],
            device_id={"exp": peer}, device_id_type=MESH)

    def reduce_turn(a, number):
        _, _, start, tall, rest = spans[number]
        wide = half // 3
        for turn, onward, by, offset in (("turn_up", "sum_up", nxt, 0), ("turn_down", "sum_down", prv, half)):
            reducer(a, number, turn).wait_recv()
            rows = pl.ds(pl.multiple_of(start + by * tall, MAIN), tall)

            def columns(i):
                cols = pl.ds(pl.multiple_of(offset + i * wide, 128), wide)
                mine = partial[a, rows, cols].astype(F32) + turned[a, rest : rest + tall, cols].astype(F32)
                partial[a, rows, cols] = mine.astype(BF)

            each(0, 3, columns)
            reducer(a, number, onward).start()

    def finish(number):
        _, _, start, tall, rest = spans[number]
        for a in range(2):
            for which in ("own_up", "own_down", "sum_up", "sum_down"):
                reducer(a, number, which).wait_recv()
        rows = pl.ds(pl.multiple_of(start + level * tall, MAIN), tall)
        there = pl.ds(rest, tall)

        def columns(i):
            cols = pl.ds(pl.multiple_of(i * 384, 128), 384)

            def total(a):
                return (partial[a, rows, cols].astype(F32) + below[a, there, cols].astype(F32)
                        + above[a, there, cols].astype(F32))

            pre = total(1)
            sigma = jax.nn.sigmoid(pre)
            slope[rows, cols] = (total(0) * (sigma * (1.0 + pre * (1.0 - sigma)))).astype(BF)

        each(0, hidden // 384, columns)
        for which in ("up_low", "down_high", "up_high", "down_low"):
            spread(number, which).start()

    def spread(number, which):
        _, _, start, tall, _ = spans[number]

        def owned(by):
            return pl.ds(pl.multiple_of(start + by * tall, MAIN), tall)

        owner, cols, peer = {
            "up_low": (level, low, nxt),
            "up_high": (level, high, nxt),
            "down_high": (level, high, prv),
            "down_low": (level, low, prv),
            "on_up": (prv, low, nxt),
            "on_down": (nxt, high, prv),
        }[which]
        slot = ("up_low", "up_high", "down_high", "down_low", "on_up", "on_down").index(which)
        rows = slope.at[owned(owner), cols]
        return pltpu.make_async_remote_copy(
            src_ref=rows, dst_ref=rows,
            send_sem=gather_s.at[number, slot], recv_sem=gather_r.at[number, slot],
            device_id={"exp": peer}, device_id_type=MESH)

    def spread_on(number):
        spread(number, "up_low").wait_recv()
        spread(number, "on_up").start()
        spread(number, "down_high").wait_recv()
        spread(number, "on_down").start()

    def spread_done(number):
        for which in ("up_high", "down_low", "on_up", "on_down"):
            spread(number, which).wait_recv()

    def cross(number, side, piece):
        _, _, start, tall, rest = spans[number]
        cols = pl.ds(piece * (group // 2), group // 2)
        return pltpu.make_async_remote_copy(
            src_ref=back.at[pl.ds(pl.multiple_of(start + side * 2 * tall, MAIN), 2 * tall), cols],
            dst_ref=crossed.at[pl.ds(2 * rest, 2 * tall), cols],
            send_sem=cross_s.at[number, piece], recv_sem=cross_r.at[number, piece],
            device_id={"ctx": partner}, device_id_type=MESH)

    def expert_back(number, pieces_of=(0, 1)):
        _, _, start, tall, _ = spans[number]

        def columns(i):
            at = pl.multiple_of(i * 256, 256)
            product = nt(slope[start : start + 4 * tall, :], up[pl.ds(at, 256), :])
            back[start : start + 4 * tall, pl.ds(at, 256)] = product.astype(BF)

        for piece in pieces_of:
            each(piece * 3, piece * 3 + 3, columns)
            cross(number, 1 - core, piece).start()

    def go_home(k):
        number = sum(k >= first_k for first_k, *_ in spans) - 1
        first_k, n, _, tall, rest = spans[number]
        owner, place_in = divmod(k - first_k, n // 2)
        row = 2 * rest + owner * tall + place_in * MAIN
        return pltpu.make_async_remote_copy(
            src_ref=final.at[pl.ds(row, MAIN), :], dst_ref=home.at[slot_rows(chip), :],
            send_sem=home_s.at[0], recv_sem=home_r.at[0],
            device_id={"ctx": from_chip(k)}, device_id_type=MESH)

    def home_all():
        rows = pl.ds(0, (chips - 1) * MAIN)
        return pltpu.make_async_remote_copy(
            src_ref=final.at[rows, :], dst_ref=home.at[rows, :], send_sem=home_s.at[0], recv_sem=home_r.at[0],
            device_id={"ctx": partner}, device_id_type=MESH)

    def extra_home(k):
        return pltpu.make_async_remote_copy(
            src_ref=home_extra_out.at[k], dst_ref=home_extra.at[chip],
            send_sem=homex_s.at[0], recv_sem=homex_r.at[0],
            device_id={"ctx": from_chip(k)}, device_id_type=MESH)

    def extra_home_all():
        rows = pl.ds(0, chips - 1)
        return pltpu.make_async_remote_copy(
            src_ref=home_extra_out.at[rows], dst_ref=home_extra.at[rows],
            send_sem=homex_s.at[0], recv_sem=homex_r.at[0],
            device_id={"ctx": partner}, device_id_type=MESH)

    def return_rows(number):
        first_k, n, start, tall, rest = spans[number]
        own = pl.multiple_of(start + core * 2 * tall, MAIN)
        for piece in range(2):
            cross(number, core, piece).wait_recv()

            def columns(i):
                cols = pl.ds(pl.multiple_of(i * 256, 256), 256)
                mine = back[pl.ds(own, 2 * tall), cols].astype(F32)
                mine += crossed[2 * rest : 2 * rest + 2 * tall, cols].astype(F32)
                final[2 * rest : 2 * rest + 2 * tall, cols] = mine.astype(BF)

            each(piece * 3, piece * 3 + 3, columns)
        if number == EXTRAS:
            count = chips * EXTRA
            row, col = iota((chips * 8, count), 1), iota((chips * 8, count), 0)
            origin = lax.div(row, 2) * 8 + lax.rem(row, 2)
            total = jnp.zeros((chips * 8, quarter), F32)
            for q in range(QUARTERS):
                cols = slice(q * quarter, (q + 1) * quarter)
                spare = jnp.concatenate(
                    [final[2 * rest + (o + 1) * tall - MAIN : 2 * rest + (o + 1) * tall, cols] for o in range(2)], axis=0)
                total += nn((col == origin + EXTRA * q).astype(F32).astype(BF), spare)
            home_extra_out[...] = total.astype(BF).reshape(chips, 8, quarter)
            for k in range(chips):
                if k != OWN:
                    extra_home(k).start()
            home_extra[chip] = home_extra_out[OWN]
        for k in chunk_slots(number):
            if k != OWN:
                go_home(k).start()
            else:
                owner, place_in = divmod(k - first_k, n // 2)
                row = 2 * rest + owner * tall + place_in * MAIN
                home[slot_rows(chip), :] = final[row : row + MAIN, :]

    part = heads * DH // 2
    pieces = part // chips
    half_mine = pl.ds(pl.multiple_of(core * part, MAIN), part)
    half_other = pl.ds(pl.multiple_of((1 - core) * part, MAIN), part)

    class Scan:
        def __init__(self, reverse, own, result, swap, summed, got, made, prefix, onward, send, recv):
            self.reverse, self.own, self.result = reverse, own, result
            self.swap, self.summed, self.got, self.made = swap, summed, got, made
            self.prefix, self.onward, self.send, self.recv = prefix, onward, send, recv
            self.leads = core == (1 if reverse else 0)

        def trade(self):
            return pltpu.make_async_remote_copy(
                src_ref=self.own.at[half_other, :], dst_ref=self.swap, send_sem=self.send.at[0], recv_sem=self.recv.at[0],
                device_id={"ctx": partner}, device_id_type=MESH)

        def piece(self, number):
            return pl.ds(pl.multiple_of(number * pieces, MAIN), pieces)

        def out(self, stage, k):
            peer = lax.rem(chip + k, chips)
            source, target = ((self.summed, self.got), (self.made, self.prefix))[stage]
            return pltpu.make_async_remote_copy(
                src_ref=source.at[self.piece(peer), :], dst_ref=target.at[self.piece(chip), :],
                send_sem=self.send.at[1 + stage], recv_sem=self.recv.at[1 + stage],
                device_id={"ctx": peer * 2 + core}, device_id_type=MESH)

        def whole(self, stage):
            source, target = ((self.summed, self.got), (self.made, self.prefix))[stage]
            rows = pl.ds(0, (chips - 1) * pieces)
            return pltpu.make_async_remote_copy(
                src_ref=source.at[rows, :], dst_ref=target.at[rows, :],
                send_sem=self.send.at[1 + stage], recv_sem=self.recv.at[1 + stage],
                device_id={"ctx": partner}, device_id_type=MESH)

        def hand(self):
            return pltpu.make_async_remote_copy(
                src_ref=self.onward, dst_ref=self.result.at[half_mine, :], send_sem=self.send.at[3], recv_sem=self.recv.at[3],
                device_id={"ctx": partner}, device_id_type=MESH)

        def lead_rows(self, j):
            rows = pl.ds(j * DH, DH)
            own = self.own[pl.ds(pl.multiple_of(core * part + j * DH, DH), DH), :].astype(F32)
            other = self.swap[rows, :].astype(F32)
            fade = jnp.exp(jnp.full((DH, DH), -rates[core * (heads // 2) + j] * float(block), F32))
            first_one = jnp.where(self.leads, own, other)
            return rows, own, other, fade, first_one

        def join(self):
            self.trade().wait_recv()
            for j in range(heads // 2):
                rows, own, other, fade, first_one = self.lead_rows(j)
                self.summed[rows, :] = (fade * first_one + jnp.where(self.leads, other, own)).astype(BF)
            each(1, chips, lambda k: self.out(0, k).start())
            self.got[self.piece(chip), :] = self.summed[self.piece(chip), :]

        def run(self):
            row = iota((pieces, DH), 0) + chip * pieces
            rate = jnp.zeros((pieces, DH), F32)
            for j in range(heads // 2):
                rate = jnp.where((row >= j * DH) & (row < (j + 1) * DH), rates[core * (heads // 2) + j], rate)
            factor = jnp.exp(-rate * float(2 * block))
            self.whole(0).wait_recv()
            total = jnp.zeros((pieces, DH), F32)
            for i in range(chips):
                c = chips - 1 - i if self.reverse else i
                self.made[c * pieces : (c + 1) * pieces, :] = total.astype(BF)
                total = factor * total + self.got[c * pieces : (c + 1) * pieces, :].astype(F32)
            each(1, chips, lambda k: self.out(1, k).start())
            self.prefix[self.piece(chip), :] = self.made[self.piece(chip), :]

        def split(self):
            self.whole(1).wait_recv()
            for j in range(heads // 2):
                rows, _, _, fade, first_one = self.lead_rows(j)
                here = self.prefix[rows, :].astype(F32)
                after = fade * here + first_one
                self.onward[rows, :] = jnp.where(self.leads, after, here).astype(BF)
                target = pl.ds(pl.multiple_of(core * part + j * DH, DH), DH)
                self.result[target, :] = jnp.where(self.leads, here, after).astype(BF)
            self.hand().start()

        def done(self):
            self.hand().wait_recv()

        def sent(self):
            self.trade().wait_send()
            self.whole(0).wait_send()
            self.whole(1).wait_send()
            self.hand().wait_send()

    fore = Scan(False, local, entering, swap, summed, got, made, prefix, onward, fore_s, fore_r)
    rear = Scan(True, local_b, leaving, swap_b, summed_b, got_b, made_b, prefix_b, onward_b, rear_s, rear_r)
    place = iota((block, DH), 0).astype(F32)

    def write_out(i):
        source, target = ((query_g, query_out), (key_g, key_out), (value_g, value_out))[i]
        return pltpu.make_async_copy(source, target, out_sem.at[i])

    def head_cols(h):
        return slice(h * DH, (h + 1) * DH)

    def scan_trade(path):
        path.trade().start()

    def scan_join(path):
        path.join()

    def scan_run(path):
        path.run()

    def scan_split(path):
        path.split()

    def scan_done(path):
        path.done()

    def within(h):
        distance = (iota((block, block), 0) - iota((block, block), 1)).astype(F32)
        return jnp.where(distance >= 0.0, jnp.exp(-rates[h] * jnp.maximum(distance, 0.0)), 0.0)

    loads[1].wait()
    gather(0, out_grad)
    for i in (2, 3, 4):
        loads[i].wait()
    for h in range(heads):
        faded = (keys[:, head_cols(h)].astype(F32) * jnp.exp(-rates[h] * (float(block) - place))).astype(BF)
        local[h * DH : (h + 1) * DH, :] = tn(faded, values[:, head_cols(h)]).astype(BF)
    pl.semaphore_wait(barrier, ctx - 1 + 2)
    scan_trade(fore)
    for i in (5, 6):
        loads[i].wait()
    for k in range(2):
        gates[:, k : k + 1] = upright(gate_rows[k : k + 1, :])

    def inside(h):
        score = nt(queries[:, head_cols(h)], keys[:, head_cols(h)])
        weight = (scale * score * within(h)).astype(BF)
        weights[h] = weight
        intra[:, head_cols(h)] = nn(weight, values[:, head_cols(h)])

    for h in range(heads // 2):
        inside(h)
    scan_join(fore)
    send_rows(0, MID)
    for h in range(heads // 2, heads):
        inside(h)
    scan_run(fore)
    send_rows(0, NEAR)
    pass_on(0, MID)
    send_rows(0, FAR)
    all_rows(0, MID)
    loads[7].wait()
    expert_in(0, MID)
    pass_on(0, NEAR)
    scan_split(fore)
    all_rows(0, NEAR)
    scan_done(fore)
    for h in range(heads):
        across = nn(queries[:, head_cols(h)], entering[h * DH : (h + 1) * DH, :])
        total = intra[:, head_cols(h)] + scale * jnp.exp(-rates[h] * place) * across
        attn[:, head_cols(h)] = total.astype(BF)
    gather(1, attn)
    send_rows(1, FAR)
    send_rows(1, MID)
    send_rows(1, NEAR)
    reduce_turn(0, MID)
    expert_in(0, NEAR)
    pass_on(0, FAR)
    all_rows(0, FAR)
    expert_in(0, FAR)
    reduce_turn(0, NEAR)
    pass_on(1, FAR)
    all_rows(1, FAR)
    loads[8].wait()
    expert_in(1, FAR)
    reduce_turn(0, FAR)
    pass_on(1, MID)
    all_rows(1, MID)
    expert_in(1, MID)
    pass_on(1, NEAR)
    reduce_turn(1, FAR)
    all_rows(1, NEAR)
    expert_in(1, NEAR)
    reduce_turn(1, MID)
    finish(FAR)
    reduce_turn(1, NEAR)
    spread_on(FAR)
    finish(MID)
    spread_done(FAR)
    spread_on(MID)
    finish(NEAR)
    expert_back(FAR)
    return_rows(FAR)
    spread_done(MID)
    expert_back(MID, (0,))
    spread_on(NEAR)
    expert_back(MID, (1,))
    return_rows(MID)
    for a in range(2):
        dispatch_extra_all(a).wait_send()
        relay_extra(a).wait_send()
        sent = send_main.at[a, pl.ds(0, (chips - 1) * MAIN), :]
        pltpu.make_async_remote_copy(
            src_ref=sent, dst_ref=sent, send_sem=main_s.at[a], recv_sem=main_r.at[a, 0],
            device_id={"ctx": partner}, device_id_type=MESH).wait_send()
        for number in range(len(CHUNKS)):
            relay_all(a, number).wait_send()
            for which in ("turn_up", "turn_down", "own_up", "own_down", "sum_up", "sum_down"):
                reducer(a, number, which).wait_send()
    fore.sent()
    spread_done(NEAR)
    expert_back(NEAR)
    return_rows(NEAR)

    extra_home_all().wait_recv()
    home_all().wait_recv()
    for q in range(QUARTERS):
        cols = slice(q * quarter, (q + 1) * quarter)
        total = out_grad[:, cols].astype(F32)
        for k in range(2):
            mine = nn(main_hot[k], home[:, cols])
            mine += nn(extra_hot[k, q], home_extra[...].reshape(chips * 8, quarter))
            total += gates[:, k : k + 1] * mine
        grad_out[:, cols] = total.astype(BF)
    for h in range(heads):
        faded = (queries[:, head_cols(h)].astype(F32) * jnp.exp(-rates[h] * (place + 1.0))).astype(BF)
        local_b[h * DH : (h + 1) * DH, :] = tn(faded, grad_out[:, head_cols(h)]).astype(BF)
    scan_trade(rear)
    for h in range(heads):
        if h == heads // 3:
            scan_join(rear)
        cols = head_cols(h)
        grad = grad_out[:, cols]
        dweight = (scale * nt(grad, values[:, cols]) * within(h)).astype(BF)
        across = nt(grad, entering[h * DH : (h + 1) * DH, :])
        query_g[:, cols] = (nn(dweight, keys[:, cols]) + scale * jnp.exp(-rates[h] * place) * across).astype(BF)
        key_part[:, cols] = tn(dweight, queries[:, cols])
        value_part[:, cols] = tn(weights[h], grad)
    write_out(0).start()
    scan_run(rear)
    extra_home_all().wait_send()
    home_all().wait_send()
    for number in range(len(CHUNKS)):
        for piece in range(2):
            cross(number, 1 - core, piece).wait_send()
        for which in ("up_low", "up_high", "down_high", "down_low", "on_up", "on_down"):
            spread(number, which).wait_send()
    for h in range(heads):
        cols = head_cols(h)
        fade = scale * jnp.exp(-rates[h] * (float(block) - 1.0 - place))
        attn[:, cols] = (fade * values[:, cols].astype(F32)).astype(BF)
        faded_keys[:, cols] = (fade * keys[:, cols].astype(F32)).astype(BF)
    scan_split(rear)
    scan_done(rear)
    for h in range(heads):
        cols = head_cols(h)
        state = leaving[h * DH : (h + 1) * DH, :]
        key_g[:, cols] = (key_part[:, cols] + nt(attn[:, cols], state)).astype(BF)
    write_out(1).start()
    for h in range(heads):
        cols = head_cols(h)
        state = leaving[h * DH : (h + 1) * DH, :]
        value_g[:, cols] = (value_part[:, cols] + nn(faded_keys[:, cols], state)).astype(BF)
    write_out(2).start()
    for i in range(3):
        write_out(i).wait()

    rear.sent()


def leave_kernel(first, second, third, first_out, second_out, third_out, sems):
    copies = [
        pltpu.make_async_copy(source, target, sems.at[i])
        for i, (source, target) in enumerate(((first, first_out), (second, second_out), (third, third_out)))
    ]
    for copy in copies:
        copy.start()
    for copy in copies:
        copy.wait()


def on_device(
    queries, keys, values, out_grad, up_weight, down_weight, decay_rates, routes, gate_weights
):
    block, group = queries.shape
    heads = group // DH
    hidden = up_weight.shape[2]
    ctx = lax.axis_size("ctx")
    chips = ctx // 2
    slots = chips * MAIN
    total = 2 * chips * (MAIN + EXTRA)
    quarter = group // QUARTERS
    count = len(CHUNKS)
    state = (heads * DH, DH)
    dma = pltpu.SemaphoreType.DMA
    raw = pl.BlockSpec(memory_space=pl.ANY)
    kept = pl.BlockSpec(memory_space=pltpu.HBM)
    out = jax.ShapeDtypeStruct((block, group), BF)
    grads = pl.pallas_call(
        layer_kernel,
        out_shape=(out, out, out),
        in_specs=[raw] * 9,
        out_specs=(raw, raw, raw),
        scratch_shapes=[pltpu.VMEM((block, group), BF)] * 3
        + [
            pltpu.SMEM((heads,), F32),
            pltpu.VMEM((2, block), jnp.int32),
            pltpu.VMEM((2, block), F32),
        ]
        + [pltpu.VMEM((block, group), BF)] * 4
        + [
            pltpu.VMEM((block, 2), F32),
            pltpu.VMEM((group, hidden), BF),
            pltpu.VMEM((hidden, group), BF),
            pltpu.VMEM((2, block, slots), BF),
            pltpu.VMEM((2, QUARTERS, block, chips * 8), BF),
            pltpu.VMEM((slots, block), BF),
            pltpu.VMEM((QUARTERS, chips * 8, block), BF),
            pltpu.VMEM((2, slots, group), BF),
            pltpu.VMEM((2, chips, 8, quarter), BF),
            pltpu.VMEM((2, total, group), BF),
            pltpu.VMEM((2, 2 * chips, 8, quarter), BF),
            pltpu.VMEM((2, total, hidden), BF),
            pltpu.VMEM((2, total // 4, hidden), BF),
            pltpu.VMEM((2, total // 4, hidden), BF),
            pltpu.VMEM((2, total // 4, hidden), BF),
            pltpu.VMEM((total, hidden), BF),
            pltpu.VMEM((total, group), BF),
            pltpu.VMEM((total // 2, group), BF),
            pltpu.VMEM((total // 2, group), BF),
            pltpu.VMEM((chips, 8, quarter), BF),
            pltpu.VMEM((slots, group), BF),
            pltpu.VMEM((chips, 8, quarter), BF),
            pltpu.VMEM((heads, block, block), BF),
            pltpu.VMEM((block, group), F32),
            pltpu.VMEM((block, group), BF),
        ]
        + [pltpu.VMEM(state, BF)] * 4
        + [pltpu.VMEM((heads * DH // 2, DH), BF)] * 12
        + [
            pltpu.VMEM((block, group), BF),
            pltpu.VMEM((block, group), F32),
            pltpu.VMEM((block, group), F32),
            pltpu.VMEM((block, group), BF),
            dma((9,)), dma((3,)),
            dma((2,)), dma((2, chips)),
            dma((2, count)), dma((2, count)),
        ]
        + [dma((2,))] * 4
        + [dma((4,))] * 4
        + [dma((2, count, 6))] * 2
        + [dma((count, 6))] * 2
        + [dma((count, 2))] * 2
        + [dma((1,))] * 4,
        compiler_params=pltpu.CompilerParams(
            collective_id=0, has_side_effects=True, vmem_limit_bytes=55250000
        ),
    )(decay_rates, routes.T, gate_weights.T, queries, keys, values, out_grad, up_weight, down_weight)
    return pl.pallas_call(
        leave_kernel,
        out_shape=(out, out, out),
        in_specs=[raw] * 3,
        out_specs=(kept, kept, kept),
        scratch_shapes=[dma((3,))],
        compiler_params=pltpu.CompilerParams(vmem_limit_bytes=1 << 20),
    )(*grads)


def solution(mesh):
    placed = (
        P("ctx", "exp"),
        P("ctx", "exp"),
        P("ctx", "exp"),
        P("ctx", "exp"),
        P("ctx", "exp", None),
        P("ctx", None, "exp"),
        P("exp"),
        P("ctx", None),
        P("ctx", None),
    )
    return jax.shard_map(
        on_device,
        mesh=mesh,
        in_specs=placed,
        out_specs=(P("ctx", "exp"), P("ctx", "exp"), P("ctx", "exp")),
        check_vma=False,
    )
```
